256 devices in a mesh: seq: 32 (over y, z), grp: 8 (over x, core).
Axes of the slice: x: 4, y: 4, z: 8, core: 2. Of those that a mesh axis runs over, the one named last changes fastest.
Arguments:
- mixer_input: bfloat16 [5120, 32768], P('grp', 'seq'), may hold values from -5 to 5
- step_sizes: float32 [80, 32768], P('grp', 'seq'), may hold values from 0 to 1, as said below
- decay_rates: float32 [80], P('grp'), may hold values from 1 to 2
- skip_gain: float32 [80], P('grp'), may hold values from 0.5 to 1.5
- input_basis: bfloat16 [32768, 128], P('seq'), may hold values from -5 to 5
- output_basis: bfloat16 [32768, 128], P('seq'), may hold values from -0.5 to 0.5
- out_weight: bfloat16 [5120, 2560], P(None, 'grp'), may hold values from -0.078125 to 0.078125
Outputs:
- layer_output: bfloat16 [32768, 2560], P('seq', 'grp')
The draws below stay inside these ranges and needn't reach their ends.
Inputs may be any that keep to these rules, and one draw needn't show every extreme that they name: `step_sizes`: positive step sizes.
All inputs are finite; a program needn't handle non-finite values.
Results may differ from the reference program's by a relative error of at most 0.0065.
Values may be sent and summed in bfloat16 or wider, within the bound.
A program may use at most 128 MiB of HBM per device.

```python
import math
import jax
import jax.numpy as jnp
from jax import lax

D = 2560
NH = 80
HP = 64
N = 128
GROUP = 256
TOK_DEV = 1024
DI = 5120
LENGTH = 32768


def draw_step_sizes(key, part):
    keys = jax.random.split(key, 5)
    quick_share = 0.4
    middle_share = 0.6
    chooser = jax.random.uniform(keys[0], (NH,))
    base_step = jnp.where(chooser < quick_share, 1.0 / 32.0, jnp.where(chooser < middle_share, 0.5 / GROUP, 0.6 / TOK_DEV))
    jitter = jax.random.uniform(keys[1], (NH, LENGTH), minval=0.5, maxval=1.5)
    block_factor = jnp.exp(jax.random.uniform(keys[2], (NH, LENGTH // GROUP), minval=-0.7, maxval=0.7))
    block_factor = jnp.repeat(block_factor, GROUP, axis=1)
    shard_factor = jnp.exp(jax.random.uniform(keys[3], (NH, LENGTH // TOK_DEV), minval=-0.8, maxval=0.8))
    shard_factor = jnp.repeat(shard_factor, TOK_DEV, axis=1)
    spike_places = jax.random.randint(keys[4], (NH, 3, 1), 0, LENGTH)
    positions = jnp.arange(LENGTH)[None, None, :]
    spikes = jnp.sum((positions == spike_places).astype(jnp.float32), axis=1)
    values = base_step[:, None] * jitter * block_factor * shard_factor + 0.3 * spikes
    return jnp.minimum(values, 0.95).astype(jnp.float32)


def draw_mixer_input(key, part):
    keys = jax.random.split(jax.random.fold_in(key, 11), 2)
    rough = jax.random.truncated_normal(keys[0], -4.0, 4.0, (DI, LENGTH))
    offset = jax.random.uniform(keys[1], (DI, 1), minval=-1.0, maxval=1.0)
    return (rough + offset).astype(jnp.bfloat16)


def draw_input_basis(key, part):
    keys = jax.random.split(jax.random.fold_in(key, 23), 2)
    rough = jax.random.truncated_normal(keys[0], -4.0, 4.0, (LENGTH, N))
    offset = jax.random.uniform(keys[1], (1, N), minval=-1.0, maxval=1.0)
    return (rough + offset).astype(jnp.bfloat16)


def levels(rng, extent, shards, least, largest):
    factor_of, own = 1.0, jax.random.fold_in(rng, 6)
    for position, shards_of in shards:
        steps = jnp.exp(jax.random.uniform(jax.random.fold_in(own, position), (shards_of,), jnp.float32, least / len(shards), largest / len(shards)))
        factor_of = factor_of * jnp.repeat(steps, extent[position] // shards_of).reshape([-1 if axis == position else 1 for axis in range(len(extent))])
    return factor_of


def centred(stream_key, shape, deviation, bound, cuts=(), kind=jnp.bfloat16):
    level = levels(stream_key, shape, cuts, -0.22, 0.18) if cuts else 1.0
    array = jax.random.normal(stream_key, shape, jnp.float32) * deviation * level
    return jnp.minimum(jnp.maximum(array, -bound), bound).astype(kind)


def setup_inputs(seed: int = 0) -> dict:
    key_of = jax.random.split(jax.random.key(seed), 8)
    mixer_input = draw_mixer_input(jax.random.fold_in(key_of[7], 71), 0)
    step_sizes = draw_step_sizes(jax.random.fold_in(key_of[7], 71), 0)
    decay_rates = jnp.clip(jnp.exp(math.log(2.0) - 0.6931472 * jax.random.uniform(key_of[2], (NH,), jnp.float32) ** levels(key_of[2], (NH,), ((0, 8),), -0.2, 0.2)), 1.0, 2.0)
    skip_gain = jnp.clip(0.5 + 1.0 * jax.random.uniform(key_of[3], (NH,), jnp.float32) ** levels(key_of[3], (NH,), ((0, 8),), -0.2, 0.2), 0.5, 1.5)
    input_basis = draw_input_basis(jax.random.fold_in(key_of[7], 71), 0)
    output_basis = centred(key_of[5], (LENGTH, N), N ** -0.5, 0.5, ((0, 32),))
    out_weight = centred(key_of[6], (DI, D), DI ** -0.5, 0.078125, ((1, 8),))
    return dict(mixer_input=mixer_input, step_sizes=step_sizes, decay_rates=decay_rates, skip_gain=skip_gain, input_basis=input_basis, output_basis=output_basis, out_weight=out_weight)


def reference(mixer_input, step_sizes, decay_rates, skip_gain, input_basis, output_basis, out_weight):
    count = LENGTH // GROUP
    inputs_blocked = mixer_input.T.reshape(count, GROUP, NH, HP)
    log_decay = -(decay_rates[:, None] * step_sizes)
    decay_blocked = log_decay.reshape(NH, count, GROUP).transpose(1, 0, 2)
    steps_blocked = step_sizes.reshape(NH, count, GROUP).transpose(1, 0, 2)
    basis_in_blocked = input_basis.reshape(count, GROUP, N)
    output_basis_grouped = output_basis.reshape(count, GROUP, N)
    rows_index = lax.broadcasted_iota(jnp.int32, (GROUP, GROUP), 0)
    cols_index = lax.broadcasted_iota(jnp.int32, (GROUP, GROUP), 1)
    causal = (rows_index >= cols_index)[None]

    def advance(state, items):
        block_input, block_decay, block_steps, basis_in, basis_out = items
        running = jnp.cumsum(block_decay, axis=1)
        gram = jnp.dot(basis_out, basis_in.T, preferred_element_type=jnp.float32)
        gaps = running[:, :, None] - running[:, None, :]
        mixing = jnp.where(causal, gram[None] * jnp.exp(jnp.where(causal, gaps, 0.0)) * block_steps[:, None, :], 0.0).astype(jnp.bfloat16)
        inner = jnp.einsum('hij,jhp->ihp', mixing.astype(jnp.float32), block_input.astype(jnp.float32), precision=lax.Precision.HIGHEST)
        tail = jnp.exp(running[:, -1:] - running) * block_steps
        weighted_terms = (basis_in.astype(jnp.float32)[None] * tail[:, :, None]).astype(jnp.bfloat16)
        digest_record = jnp.einsum('hjn,jhp->hnp', weighted_terms.astype(jnp.float32), block_input.astype(jnp.float32), precision=lax.Precision.HIGHEST)
        from_state = jnp.einsum('in,hnp->ihp', basis_out.astype(jnp.float32), state, precision=lax.Precision.HIGHEST)
        from_state = from_state * jnp.exp(running).T[:, :, None]
        mixed = inner + from_state + skip_gain[None, :, None] * block_input.astype(jnp.float32)
        new_state = jnp.exp(running[:, -1])[:, None, None] * state + digest_record
        return new_state, mixed.astype(jnp.bfloat16)

    start_state = jnp.zeros((NH, N, HP), jnp.float32)
    _, outputs = lax.scan(advance, start_state, (inputs_blocked, decay_blocked, steps_blocked, basis_in_blocked, output_basis_grouped))
    mixed_all = outputs.reshape(LENGTH, NH * HP)
    return jnp.dot(mixed_all, out_weight, preferred_element_type=jnp.float32).astype(jnp.bfloat16)
```

```python
import jax
import jax.numpy as jnp
from jax import lax
from jax.sharding import PartitionSpec as P

HP = 64
N = 128
GROUP = 256


def carry_in(total_log, final_state):
    peers, here = lax.axis_size("seq"), lax.axis_index("seq")

    def shifted(value, d):
        return lax.ppermute(value, "seq", [(i, i + d) for i in range(peers - d)])

    decay = shifted(jnp.exp(total_log), 1)
    decay = jnp.where(here >= 1, decay, jnp.ones_like(decay))
    state = shifted(final_state, 1)
    d = 1
    while d < peers:
        decay_r, state_r = shifted(decay, d), shifted(state, d)
        reached = here >= d
        state = jnp.where(reached, decay[:, None, None] * state_r + state, state)
        decay = jnp.where(reached, decay * decay_r, decay)
        d *= 2
    return state


def on_device(
    mixer_input, step_sizes, decay_rates, skip_gain, input_basis, output_basis, out_weight
):
    heads_here = step_sizes.shape[0]
    tokens_here = step_sizes.shape[1]
    count = tokens_here // GROUP
    channels = mixer_input.reshape(heads_here, HP, count, GROUP)
    log_decay = -(decay_rates[:, None] * step_sizes).reshape(heads_here, count, GROUP)
    steps_blocked = step_sizes.reshape(heads_here, count, GROUP)
    running = jnp.cumsum(log_decay, axis=2)
    basis_in_blocked = input_basis.reshape(count, GROUP, N)
    basis_out_blocked = output_basis.reshape(count, GROUP, N)
    gram = jnp.einsum(
        "cin,cjn->cij", basis_out_blocked, basis_in_blocked, preferred_element_type=jnp.float32
    )
    rows_index = lax.broadcasted_iota(jnp.int32, (GROUP, GROUP), 0)
    cols_index = lax.broadcasted_iota(jnp.int32, (GROUP, GROUP), 1)
    causal = rows_index >= cols_index
    gaps = running[:, :, :, None] - running[:, :, None, :]
    mixing = jnp.where(
        causal,
        gram[None] * jnp.exp(jnp.where(causal, gaps, 0.0)) * steps_blocked[:, :, None, :],
        0.0,
    ).astype(jnp.bfloat16)
    inner = jnp.einsum("hcij,hpcj->hpci", mixing, channels, preferred_element_type=jnp.float32)
    tail = jnp.exp(running[:, :, -1:] - running) * steps_blocked
    weighted_terms = (basis_in_blocked.astype(jnp.float32)[None] * tail[:, :, :, None]).astype(
        jnp.bfloat16
    )
    summaries = jnp.einsum(
        "hcjn,hpcj->chnp", weighted_terms, channels, preferred_element_type=jnp.float32
    )
    block_decay = jnp.exp(running[:, :, -1])

    def advance(state, pair):
        decay, digest_record = pair
        return (decay[:, None, None] * state + digest_record, state)

    zero_state = jnp.zeros((heads_here, N, HP), jnp.float32)
    final_state, entering = lax.scan(advance, zero_state, (block_decay.T, summaries))
    block_sums = jnp.sum(log_decay, axis=2)
    prefix = jnp.exp(jnp.cumsum(block_sums, axis=1) - block_sums)
    total_log = jnp.sum(block_sums, axis=1)
    basis_out_wide = basis_out_blocked.astype(jnp.float32)
    within = jnp.exp(running)[:, None]
    direct = skip_gain[:, None, None, None] * channels.astype(jnp.float32)
    carried = carry_in(total_log, final_state)
    states = entering + prefix.T[:, :, None, None] * carried[None]
    from_state = jnp.einsum(
        "cin,chnp->hpci", basis_out_wide, states, precision=lax.Precision.HIGHEST
    )
    mixed = inner + from_state * within + direct
    mixed_columns = mixed.astype(jnp.bfloat16).reshape(heads_here * HP, tokens_here)
    result = jnp.einsum(
        "kt,kd->td",
        lax.all_gather(mixed_columns, "grp", axis=0, tiled=True),
        out_weight,
        preferred_element_type=jnp.float32,
    )
    return result.astype(jnp.bfloat16)


def solution(mesh):
    placed = (
        P("grp", "seq"),
        P("grp", "seq"),
        P("grp"),
        P("grp"),
        P("seq", None),
        P("seq", None),
        P(None, "grp"),
    )
    return jax.shard_map(
        on_device, mesh=mesh, in_specs=placed, out_specs=P("seq", "grp"), check_vma=False
    )
```

```python
import functools

import jax
import jax.numpy as jnp
from jax import lax
from jax.experimental import pallas as pl
from jax.experimental.pallas import tpu as pltpu
from jax.sharding import PartitionSpec as P

HP = 64
N = 128
GROUP = 256


def scan_kernel(peers, names, msg_ref, out_ref, inc_ref, recv_ref, send_sem, recv_sem):
    here = lax.axis_index("seq")
    grp_here = lax.axis_index("grp")
    rows = msg_ref.shape[1] - 8

    def device(target):
        return tuple(target if name == "seq" else grp_here for name in names)

    offsets = sorted({d % peers for d in _hops(peers)} | {(-d) % peers for d in _hops(peers)})
    barrier = pltpu.get_barrier_semaphore()
    for offset in offsets:
        pl.semaphore_signal(
            barrier, inc=1, device_id=device(lax.rem(here + offset, peers)),
            device_id_type=pl.DeviceIdType.MESH,
        )
    pl.semaphore_wait(barrier, len(offsets))

    inc_ref[...] = msg_ref[...]
    out_ref[:, :rows] = jnp.zeros((out_ref.shape[0], rows, out_ref.shape[2]), jnp.float32)
    out_ref[:, rows:] = jnp.ones((out_ref.shape[0], 8, out_ref.shape[2]), jnp.float32)
    for r, d in enumerate(_hops(peers)):
        copy = pltpu.make_async_remote_copy(
            src_ref=inc_ref,
            dst_ref=recv_ref.at[r],
            send_sem=send_sem.at[r],
            recv_sem=recv_sem.at[r],
            device_id=device(lax.rem(here + d, peers)),
            device_id_type=pl.DeviceIdType.MESH,
        )
        copy.start()
        copy.wait()
        reached = here >= d
        got_state = recv_ref[r, :, :rows, :]
        got_decay = recv_ref[r, :, rows:, :]
        for ref in ((out_ref, inc_ref) if 2 * d < peers else (out_ref,)):
            decay = ref[:, rows:rows + 1, :]
            ref[:, :rows] = jnp.where(reached, decay * got_state + ref[:, :rows], ref[:, :rows])
            ref[:, rows:] = jnp.where(reached, decay * got_decay, ref[:, rows:])


def _hops(peers):
    d, hops = 1, []
    while d < peers:
        hops.append(d)
        d *= 2
    return hops


def carry_in(total_log, final_state, names):
    peers = lax.axis_size("seq")
    heads = final_state.shape[0]
    rows = N * HP // 128
    state = final_state.reshape(heads, rows, 128)
    decay = jnp.broadcast_to(jnp.exp(total_log)[:, None, None], (heads, 8, 128))
    msg = jnp.concatenate([state, decay], axis=1)
    shape = msg.shape
    out = pl.pallas_call(
        functools.partial(scan_kernel, peers, names),
        out_shape=jax.ShapeDtypeStruct(shape, jnp.float32),
        in_specs=[pl.BlockSpec(memory_space=pltpu.VMEM)],
        out_specs=pl.BlockSpec(memory_space=pltpu.VMEM),
        scratch_shapes=[
            pltpu.VMEM(shape, jnp.float32),
            pltpu.VMEM((len(_hops(peers)),) + shape, jnp.float32),
            pltpu.SemaphoreType.DMA((len(_hops(peers)),)),
            pltpu.SemaphoreType.DMA((len(_hops(peers)),)),
        ],
        compiler_params=pltpu.CompilerParams(collective_id=0, has_side_effects=True),
    )(msg)
    return out[:, :rows].reshape(heads, N, HP)


def on_device(
    names,
    mixer_input, step_sizes, decay_rates, skip_gain, input_basis, output_basis, out_weight
):
    heads_here = step_sizes.shape[0]
    tokens_here = step_sizes.shape[1]
    count = tokens_here // GROUP
    channels = mixer_input.reshape(heads_here, HP, count, GROUP)
    log_decay = -(decay_rates[:, None] * step_sizes).reshape(heads_here, count, GROUP)
    steps_blocked = step_sizes.reshape(heads_here, count, GROUP)
    running = jnp.cumsum(log_decay, axis=2)
    basis_in_blocked = input_basis.reshape(count, GROUP, N)
    basis_out_blocked = output_basis.reshape(count, GROUP, N)
    gram = jnp.einsum(
        "cin,cjn->cij", basis_out_blocked, basis_in_blocked, preferred_element_type=jnp.float32
    )
    rows_index = lax.broadcasted_iota(jnp.int32, (GROUP, GROUP), 0)
    cols_index = lax.broadcasted_iota(jnp.int32, (GROUP, GROUP), 1)
    causal = rows_index >= cols_index
    gaps = running[:, :, :, None] - running[:, :, None, :]
    mixing = jnp.where(
        causal,
        gram[None] * jnp.exp(jnp.where(causal, gaps, 0.0)) * steps_blocked[:, :, None, :],
        0.0,
    ).astype(jnp.bfloat16)
    inner = jnp.einsum("hcij,hpcj->hpci", mixing, channels, preferred_element_type=jnp.float32)
    tail = jnp.exp(running[:, :, -1:] - running) * steps_blocked
    weighted_terms = (basis_in_blocked.astype(jnp.float32)[None] * tail[:, :, :, None]).astype(
        jnp.bfloat16
    )
    summaries = jnp.einsum(
        "hcjn,hpcj->chnp", weighted_terms, channels, preferred_element_type=jnp.float32
    )
    block_decay = jnp.exp(running[:, :, -1])

    def advance(state, pair):
        decay, digest_record = pair
        return (decay[:, None, None] * state + digest_record, state)

    zero_state = jnp.zeros((heads_here, N, HP), jnp.float32)
    final_state, entering = lax.scan(advance, zero_state, (block_decay.T, summaries))
    block_sums = jnp.sum(log_decay, axis=2)
    prefix = jnp.exp(jnp.cumsum(block_sums, axis=1) - block_sums)
    total_log = jnp.sum(block_sums, axis=1)
    basis_out_wide = basis_out_blocked.astype(jnp.float32)
    within = jnp.exp(running)[:, None]
    direct = skip_gain[:, None, None, None] * channels.astype(jnp.float32)
    carried = carry_in(total_log, final_state, names)
    states = entering + prefix.T[:, :, None, None] * carried[None]
    from_state = jnp.einsum(
        "cin,chnp->hpci", basis_out_wide, states, precision=lax.Precision.HIGHEST
    )
    mixed = inner + from_state * within + direct
    mixed_columns = mixed.astype(jnp.bfloat16).reshape(heads_here * HP, tokens_here)
    result = jnp.einsum(
        "kt,kd->td",
        lax.all_gather(mixed_columns, "grp", axis=0, tiled=True),
        out_weight,
        preferred_element_type=jnp.float32,
    )
    return result.astype(jnp.bfloat16)


def solution(mesh):
    placed = (
        P("grp", "seq"),
        P("grp", "seq"),
        P("grp"),
        P("grp"),
        P("seq", None),
        P("seq", None),
        P(None, "grp"),
    )
    return jax.shard_map(
        functools.partial(on_device, mesh.axis_names), mesh=mesh, in_specs=placed, out_specs=P("seq", "grp"), check_vma=False
    )
```

```python
import functools

import jax
import jax.numpy as jnp
from jax import lax
from jax.experimental import pallas as pl
from jax.experimental.pallas import tpu as pltpu
from jax.sharding import PartitionSpec as P

HP = 64
N = 128
GROUP = 256


def scan_kernel(peers, names, msg_ref, after_ref, out_ref, inc_ref, recv_ref, send_sem, recv_sem):
    here = lax.axis_index("seq")
    grp_here = lax.axis_index("grp")
    rows = msg_ref.shape[1] - 8

    def device(target):
        return tuple(target if name == "seq" else grp_here for name in names)

    offsets = sorted({d % peers for d in _hops(peers)} | {(-d) % peers for d in _hops(peers)})
    barrier = pltpu.get_barrier_semaphore()
    for offset in offsets:
        pl.semaphore_signal(
            barrier, inc=1, device_id=device(lax.rem(here + offset, peers)),
            device_id_type=pl.DeviceIdType.MESH,
        )
    pl.semaphore_wait(barrier, len(offsets))

    inc_ref[...] = msg_ref[...]
    out_ref[:, :rows] = jnp.zeros((out_ref.shape[0], rows, out_ref.shape[2]), jnp.float32)
    out_ref[:, rows:] = jnp.ones((out_ref.shape[0], 8, out_ref.shape[2]), jnp.float32)
    for r, d in enumerate(_hops(peers)):
        copy = pltpu.make_async_remote_copy(
            src_ref=inc_ref,
            dst_ref=recv_ref.at[r],
            send_sem=send_sem.at[r],
            recv_sem=recv_sem.at[r],
            device_id=device(lax.rem(here + d, peers)),
            device_id_type=pl.DeviceIdType.MESH,
        )
        copy.start()
        copy.wait()
        reached = here >= d
        got_state = recv_ref[r, :, :rows, :]
        got_decay = recv_ref[r, :, rows:, :]
        for ref in ((out_ref, inc_ref) if 2 * d < peers else (out_ref,)):
            decay = ref[:, rows:rows + 1, :]
            ref[:, :rows] = jnp.where(reached, decay * got_state + ref[:, :rows], ref[:, :rows])
            ref[:, rows:] = jnp.where(reached, decay * got_decay, ref[:, rows:])


def _hops(peers):
    d, hops = 1, []
    while d < peers:
        hops.append(d)
        d *= 2
    return hops


def carry_in(total_log, final_state, names, after):
    peers = lax.axis_size("seq")
    heads = final_state.shape[0]
    rows = N * HP // 128
    state = final_state.reshape(heads, rows, 128)
    decay = jnp.broadcast_to(jnp.exp(total_log)[:, None, None], (heads, 8, 128))
    msg = jnp.concatenate([state, decay], axis=1)
    shape = msg.shape
    out = pl.pallas_call(
        functools.partial(scan_kernel, peers, names),
        out_shape=jax.ShapeDtypeStruct(shape, jnp.float32),
        in_specs=[pl.BlockSpec(memory_space=pltpu.VMEM), pl.BlockSpec(memory_space=pl.ANY)],
        out_specs=pl.BlockSpec(memory_space=pltpu.VMEM),
        scratch_shapes=[
            pltpu.VMEM(shape, jnp.float32),
            pltpu.VMEM((len(_hops(peers)),) + shape, jnp.float32),
            pltpu.SemaphoreType.DMA((len(_hops(peers)),)),
            pltpu.SemaphoreType.DMA((len(_hops(peers)),)),
        ],
        compiler_params=pltpu.CompilerParams(collective_id=0, has_side_effects=True),
        cost_estimate=pl.CostEstimate(flops=0, transcendentals=0, bytes_accessed=512 * msg.size * 4),
    )(msg, after)
    return out[:, :rows].reshape(heads, N, HP)


def on_device(
    names,
    mixer_input, step_sizes, decay_rates, skip_gain, input_basis, output_basis, out_weight
):
    heads_here = step_sizes.shape[0]
    tokens_here = step_sizes.shape[1]
    count = tokens_here // GROUP
    channels = mixer_input.reshape(heads_here, HP, count, GROUP)
    log_decay = -(decay_rates[:, None] * step_sizes).reshape(heads_here, count, GROUP)
    steps_blocked = step_sizes.reshape(heads_here, count, GROUP)
    running = jnp.cumsum(log_decay, axis=2)
    basis_in_blocked = input_basis.reshape(count, GROUP, N)
    basis_out_blocked = output_basis.reshape(count, GROUP, N)
    gram = jnp.einsum(
        "cin,cjn->cij", basis_out_blocked, basis_in_blocked, preferred_element_type=jnp.float32
    )
    rows_index = lax.broadcasted_iota(jnp.int32, (GROUP, GROUP), 0)
    cols_index = lax.broadcasted_iota(jnp.int32, (GROUP, GROUP), 1)
    causal = rows_index >= cols_index
    gaps = running[:, :, :, None] - running[:, :, None, :]
    mixing = jnp.where(
        causal,
        gram[None] * jnp.exp(jnp.where(causal, gaps, 0.0)) * steps_blocked[:, :, None, :],
        0.0,
    ).astype(jnp.bfloat16)
    inner = jnp.einsum("hcij,hpcj->hpci", mixing, channels, preferred_element_type=jnp.float32)
    tail = jnp.exp(running[:, :, -1:] - running) * steps_blocked
    weighted_terms = (basis_in_blocked.astype(jnp.float32)[None] * tail[:, :, :, None]).astype(
        jnp.bfloat16
    )
    summaries = jnp.einsum(
        "hcjn,hpcj->chnp", weighted_terms, channels, preferred_element_type=jnp.float32
    )
    block_decay = jnp.exp(running[:, :, -1])

    def advance(state, pair):
        decay, digest_record = pair
        return (decay[:, None, None] * state + digest_record, state)

    zero_state = jnp.zeros((heads_here, N, HP), jnp.float32)
    final_state, entering = lax.scan(advance, zero_state, (block_decay.T, summaries))
    block_sums = jnp.sum(log_decay, axis=2)
    log_prefix = jnp.cumsum(block_sums, axis=1) - block_sums
    total_log = jnp.sum(block_sums, axis=1)
    basis_out_wide = basis_out_blocked.astype(jnp.float32)
    within = jnp.exp(running)[:, None]
    direct = skip_gain[:, None, None, None] * channels.astype(jnp.float32)
    from_local = jnp.einsum(
        "cin,chnp->hpci", basis_out_wide, entering, precision=lax.Precision.HIGHEST
    )
    local = (inner + from_local * within + direct).astype(jnp.bfloat16)
    local_all = lax.all_gather(local.reshape(heads_here * HP, tokens_here), "grp", axis=0, tiled=True)
    carried = carry_in(total_log, final_state, names, local)
    scale = jnp.exp(running + log_prefix[:, :, None]).reshape(heads_here, tokens_here)
    scale_hi = scale.astype(jnp.bfloat16)
    scale_lo = (scale - scale_hi.astype(jnp.float32)).astype(jnp.bfloat16)
    message = jnp.concatenate(
        [carried.reshape(heads_here, N * HP).astype(jnp.bfloat16), scale_hi, scale_lo], axis=1
    )
    message, local_all = lax.optimization_barrier((message, local_all))
    message_all = lax.all_gather(message, "grp", axis=0, tiled=True)
    carried_all = message_all[:, : N * HP].reshape(-1, N, HP)
    scale_all = message_all[:, N * HP : N * HP + tokens_here].astype(jnp.float32) + message_all[
        :, N * HP + tokens_here :
    ].astype(jnp.float32)
    carry = jnp.einsum(
        "tn,hnp->hpt", output_basis, carried_all, preferred_element_type=jnp.float32
    ) * scale_all[:, None, :]
    mixed = (local_all.astype(jnp.float32) + carry.reshape(local_all.shape)).astype(jnp.bfloat16)
    result = jnp.einsum("kt,kd->td", mixed, out_weight, preferred_element_type=jnp.float32)
    return result.astype(jnp.bfloat16)


def solution(mesh):
    placed = (
        P("grp", "seq"),
        P("grp", "seq"),
        P("grp"),
        P("grp"),
        P("seq", None),
        P("seq", None),
        P(None, "grp"),
    )
    return jax.shard_map(
        functools.partial(on_device, mesh.axis_names), mesh=mesh, in_specs=placed, out_specs=P("seq", "grp"), check_vma=False
    )
```

```python
import functools

import jax
import jax.numpy as jnp
from jax import lax
from jax.experimental import pallas as pl
from jax.experimental.pallas import tpu as pltpu
from jax.sharding import PartitionSpec as P

HP = 64
N = 128
GROUP = 256


def scan_kernel(peers, names, msg_ref, after_ref, out_ref, inc_ref, recv_ref, send_sem, recv_sem):
    here = lax.axis_index("seq")
    grp_here = lax.axis_index("grp")
    rows = msg_ref.shape[1] - 8

    def device(target):
        return tuple(target if name == "seq" else grp_here for name in names)

    offsets = sorted({d % peers for d in _hops(peers)} | {(-d) % peers for d in _hops(peers)})
    barrier = pltpu.get_barrier_semaphore()
    for offset in offsets:
        pl.semaphore_signal(
            barrier, inc=1, device_id=device(lax.rem(here + offset, peers)),
            device_id_type=pl.DeviceIdType.MESH,
        )
    pl.semaphore_wait(barrier, len(offsets))

    inc_ref[...] = msg_ref[...]
    out_ref[:, :rows] = jnp.zeros((out_ref.shape[0], rows, out_ref.shape[2]), jnp.float32)
    out_ref[:, rows:] = jnp.ones((out_ref.shape[0], 8, out_ref.shape[2]), jnp.float32)
    for r, d in enumerate(_hops(peers)):
        copy = pltpu.make_async_remote_copy(
            src_ref=inc_ref,
            dst_ref=recv_ref.at[r],
            send_sem=send_sem.at[r],
            recv_sem=recv_sem.at[r],
            device_id=device(lax.rem(here + d, peers)),
            device_id_type=pl.DeviceIdType.MESH,
        )
        copy.start()
        copy.wait()
        reached = here >= d
        got_state = recv_ref[r, :, :rows, :]
        got_decay = recv_ref[r, :, rows:, :]
        for ref in ((out_ref, inc_ref) if 2 * d < peers else (out_ref,)):
            decay = ref[:, rows:rows + 1, :]
            ref[:, :rows] = jnp.where(reached, decay * got_state + ref[:, :rows], ref[:, :rows])
            ref[:, rows:] = jnp.where(reached, decay * got_decay, ref[:, rows:])


def _hops(peers):
    d, hops = 1, []
    while d < peers:
        hops.append(d)
        d *= 2
    return hops


def carry_in(total_log, final_state, names, after):
    peers = lax.axis_size("seq")
    heads = final_state.shape[0]
    rows = N * HP // 128
    state = final_state.reshape(heads, rows, 128)
    decay = jnp.broadcast_to(jnp.exp(total_log)[:, None, None], (heads, 8, 128))
    msg = jnp.concatenate([state, decay], axis=1)
    shape = msg.shape
    out = pl.pallas_call(
        functools.partial(scan_kernel, peers, names),
        out_shape=jax.ShapeDtypeStruct(shape, jnp.float32),
        in_specs=[pl.BlockSpec(memory_space=pltpu.VMEM), pl.BlockSpec(memory_space=pl.ANY)],
        out_specs=pl.BlockSpec(memory_space=pltpu.VMEM),
        scratch_shapes=[
            pltpu.VMEM(shape, jnp.float32),
            pltpu.VMEM((len(_hops(peers)),) + shape, jnp.float32),
            pltpu.SemaphoreType.DMA((len(_hops(peers)),)),
            pltpu.SemaphoreType.DMA((len(_hops(peers)),)),
        ],
        compiler_params=pltpu.CompilerParams(collective_id=0, has_side_effects=True),
        cost_estimate=pl.CostEstimate(flops=0, transcendentals=0, bytes_accessed=512 * msg.size * 4),
    )(msg, after)
    return out[:, :rows].reshape(heads, N, HP)


def on_device(
    names,
    mixer_input, step_sizes, decay_rates, skip_gain, input_basis, output_basis, out_weight
):
    heads_here = step_sizes.shape[0]
    tokens_here = step_sizes.shape[1]
    count = tokens_here // GROUP
    channels = mixer_input.reshape(heads_here, HP, count, GROUP)
    log_decay = -(decay_rates[:, None] * step_sizes).reshape(heads_here, count, GROUP)
    steps_blocked = step_sizes.reshape(heads_here, count, GROUP)
    running = jnp.cumsum(log_decay, axis=2)
    basis_in_blocked = input_basis.reshape(count, GROUP, N)
    basis_out_blocked = output_basis.reshape(count, GROUP, N)
    gram = jnp.einsum(
        "cin,cjn->cij", basis_out_blocked, basis_in_blocked, preferred_element_type=jnp.float32
    )
    rows_index = lax.broadcasted_iota(jnp.int32, (GROUP, GROUP), 0)
    cols_index = lax.broadcasted_iota(jnp.int32, (GROUP, GROUP), 1)
    causal = rows_index >= cols_index
    gaps = running[:, :, :, None] - running[:, :, None, :]
    mixing = jnp.where(
        causal,
        gram[None] * jnp.exp(jnp.where(causal, gaps, 0.0)) * steps_blocked[:, :, None, :],
        0.0,
    ).astype(jnp.bfloat16)
    inner = jnp.einsum("hcij,hpcj->hpci", mixing, channels, preferred_element_type=jnp.float32)
    tail_decay = jnp.exp(running[:, :, -1:] - running) * steps_blocked
    weighted_terms = (basis_in_blocked.astype(jnp.float32)[None] * tail_decay[:, :, :, None]).astype(
        jnp.bfloat16
    )
    summaries = jnp.einsum(
        "hcjn,hpcj->chnp", weighted_terms, channels, preferred_element_type=jnp.float32
    )
    block_sums = jnp.sum(log_decay, axis=2)
    block_cum = jnp.cumsum(block_sums, axis=1)
    log_prefix = block_cum - block_sums
    total_log = block_cum[:, -1]
    entering = [jnp.zeros_like(summaries[0])]
    for c in range(1, count + 1):
        reach = log_prefix[:, c] if c < count else total_log
        term = jnp.zeros_like(summaries[0])
        for earlier in range(c):
            weight = jnp.exp(reach - block_cum[:, earlier])
            term = term + weight[:, None, None] * summaries[earlier]
        entering.append(term)
    final_state = entering[count]
    entering = jnp.stack(entering[:count])
    basis_out_wide = basis_out_blocked.astype(jnp.float32)
    within = jnp.exp(running)[:, None]
    direct = skip_gain[:, None, None, None] * channels.astype(jnp.float32)
    from_local = jnp.einsum(
        "cin,chnp->hpci", basis_out_wide, entering, precision=lax.Precision.HIGHEST
    )
    local = (inner + from_local * within + direct).astype(jnp.bfloat16)
    local_all = lax.all_gather(local.reshape(heads_here * HP, tokens_here), "grp", axis=0, tiled=True)
    carried = carry_in(total_log, final_state, names, local)
    scale = jnp.exp(running + log_prefix[:, :, None]).reshape(heads_here, tokens_here)
    scale_hi = scale.astype(jnp.bfloat16)
    scale_lo = (scale - scale_hi.astype(jnp.float32)).astype(jnp.bfloat16)
    message = jnp.concatenate(
        [carried.reshape(heads_here, N * HP).astype(jnp.bfloat16), scale_hi, scale_lo], axis=1
    )
    message, local_all = lax.optimization_barrier((message, local_all))
    message_all = lax.all_gather(message, "grp", axis=0, tiled=True)
    carried_all = message_all[:, : N * HP].reshape(-1, N, HP)
    scale_all = message_all[:, N * HP : N * HP + tokens_here].astype(jnp.float32) + message_all[
        :, N * HP + tokens_here :
    ].astype(jnp.float32)
    carried_t = jnp.swapaxes(carried_all, 1, 2)
    result_t = tail(local_all, output_basis, carried_t, scale_all, out_weight.T)
    return result_t.T


def tail_kernel(local_ref, basis_ref, carried_ref, scale_ref, weight_ref, out_ref, acc_ref, mixed_ref):
    g = pl.program_id(0)

    @pl.when(g == 0)
    def _():
        acc_ref[...] = jnp.zeros_like(acc_ref)

    basis = basis_ref[...]
    for h in range(carried_ref.shape[0]):
        rows = pl.ds(h * HP, HP)
        carry = lax.dot_general(
            carried_ref[h], basis, (((1,), (1,)), ((), ())), preferred_element_type=jnp.float32
        )
        mixed_ref[rows, :] = (
            local_ref[rows, :].astype(jnp.float32) + carry * scale_ref[pl.ds(h, 1), :]
        ).astype(jnp.bfloat16)
    acc_ref[...] += jnp.dot(weight_ref[...], mixed_ref[...], preferred_element_type=jnp.float32)

    @pl.when(g == pl.num_programs(0) - 1)
    def _():
        out_ref[...] = acc_ref[...].astype(out_ref.dtype)


def tail(local_all, basis, carried_t, scale_all, weight_t):
    channels, tokens = local_all.shape
    features = weight_t.shape[0]
    heads = carried_t.shape[0]
    groups = lax.axis_size("grp")
    per = heads // groups
    return pl.pallas_call(
        tail_kernel,
        out_shape=jax.ShapeDtypeStruct((features, tokens), jnp.bfloat16),
        grid=(groups,),
        in_specs=[
            pl.BlockSpec((per * HP, tokens), lambda g: (g, 0)),
            pl.BlockSpec(basis.shape, lambda g: (0, 0)),
            pl.BlockSpec((per, HP, N), lambda g: (g, 0, 0)),
            pl.BlockSpec((None, per, tokens), lambda g: (g, 0, 0)),
            pl.BlockSpec((features, per * HP), lambda g: (0, g)),
        ],
        out_specs=pl.BlockSpec((features, tokens), lambda g: (0, 0)),
        scratch_shapes=[
            pltpu.VMEM((features, tokens), jnp.float32),
            pltpu.VMEM((per * HP, tokens), jnp.bfloat16),
        ],
        cost_estimate=pl.CostEstimate(
            flops=2 * tokens * channels * (N + features),
            transcendentals=0,
            bytes_accessed=2 * (local_all.size + weight_t.size) + 2 * features * tokens,
        ),
    )(local_all, basis, carried_t, scale_all.reshape(groups, per, tokens), weight_t)


def solution(mesh):
    placed = (
        P("grp", "seq"),
        P("grp", "seq"),
        P("grp"),
        P("grp"),
        P("seq", None),
        P("seq", None),
        P(None, "grp"),
    )
    return jax.shard_map(
        functools.partial(on_device, mesh.axis_names), mesh=mesh, in_specs=placed, out_specs=P("seq", "grp"), check_vma=False
    )
```

```python
import functools

import jax
import jax.numpy as jnp
from jax import lax
from jax.experimental import pallas as pl
from jax.experimental.pallas import tpu as pltpu
from jax.sharding import PartitionSpec as P

HP = 64
N = 128
GROUP = 256


def scan_kernel(peers, names, msg_ref, after_ref, out_ref, spread_ref, inc_ref, recv_ref, send_ref,
                send_sem, recv_sem, spread_send, spread_recv):
    here = lax.axis_index("seq")
    grp_here = lax.axis_index("grp")
    groups = spread_ref.shape[0]
    rows = msg_ref.shape[1] - 8

    def device(seq_at, grp_at):
        return tuple(seq_at if name == "seq" else grp_at for name in names)

    offsets = sorted({d % peers for d in _hops(peers)} | {(-d) % peers for d in _hops(peers)})
    barrier = pltpu.get_barrier_semaphore()
    for offset in offsets:
        pl.semaphore_signal(
            barrier, inc=1, device_id=device(lax.rem(here + offset, peers), grp_here),
            device_id_type=pl.DeviceIdType.MESH,
        )
    for offset in range(1, groups):
        pl.semaphore_signal(
            barrier, inc=1, device_id=device(here, lax.rem(grp_here + offset, groups)),
            device_id_type=pl.DeviceIdType.MESH,
        )
    pl.semaphore_wait(barrier, len(offsets) + groups - 1)

    inc_ref[...] = msg_ref[...]
    out_ref[:, :rows] = jnp.zeros((out_ref.shape[0], rows, out_ref.shape[2]), jnp.float32)
    out_ref[:, rows:] = jnp.ones((out_ref.shape[0], 8, out_ref.shape[2]), jnp.float32)
    for r, d in enumerate(_hops(peers)):
        copy = pltpu.make_async_remote_copy(
            src_ref=inc_ref,
            dst_ref=recv_ref.at[r],
            send_sem=send_sem.at[r],
            recv_sem=recv_sem.at[r],
            device_id=device(lax.rem(here + d, peers), grp_here),
            device_id_type=pl.DeviceIdType.MESH,
        )
        copy.start()
        copy.wait()
        reached = here >= d
        got_state = recv_ref[r, :, :rows, :]
        got_decay = recv_ref[r, :, rows:, :]
        for ref in ((out_ref, inc_ref) if 2 * d < peers else (out_ref,)):
            decay = ref[:, rows:rows + 1, :]
            ref[:, :rows] = jnp.where(reached, decay * got_state + ref[:, :rows], ref[:, :rows])
            ref[:, rows:] = jnp.where(reached, decay * got_decay, ref[:, rows:])

    send_ref[...] = out_ref[:, :rows].astype(send_ref.dtype)
    spread_ref[grp_here] = out_ref[:, :rows].astype(spread_ref.dtype)
    copies = []
    for offset in range(1, groups):
        copy = pltpu.make_async_remote_copy(
            src_ref=send_ref,
            dst_ref=spread_ref.at[grp_here],
            send_sem=spread_send.at[offset],
            recv_sem=spread_recv.at[grp_here],
            device_id=device(here, lax.rem(grp_here + offset, groups)),
            device_id_type=pl.DeviceIdType.MESH,
        )
        copy.start()
        copies.append(copy)
    for copy in copies:
        copy.wait_send()
    for offset in range(1, groups):
        source = lax.rem(grp_here + groups - offset, groups)
        pltpu.make_async_remote_copy(
            src_ref=send_ref,
            dst_ref=spread_ref.at[source],
            send_sem=spread_send.at[offset],
            recv_sem=spread_recv.at[source],
            device_id=device(here, source),
            device_id_type=pl.DeviceIdType.MESH,
        ).wait_recv()


def _hops(peers):
    d, hops = 1, []
    while d < peers:
        hops.append(d)
        d *= 2
    return hops


def carry_in(total_log, state_t, names, after):
    peers = lax.axis_size("seq")
    groups = lax.axis_size("grp")
    heads, rows, lanes = state_t.shape
    decay = jnp.broadcast_to(jnp.exp(total_log)[:, None, None], (heads, 8, lanes))
    msg = jnp.concatenate([state_t, decay], axis=1)
    shape = msg.shape
    hops = len(_hops(peers))
    _, spread = pl.pallas_call(
        functools.partial(scan_kernel, peers, names),
        out_shape=(
            jax.ShapeDtypeStruct(shape, jnp.float32),
            jax.ShapeDtypeStruct((groups, heads, rows, lanes), jnp.bfloat16),
        ),
        in_specs=[pl.BlockSpec(memory_space=pltpu.VMEM), pl.BlockSpec(memory_space=pl.ANY)],
        out_specs=(pl.BlockSpec(memory_space=pltpu.VMEM), pl.BlockSpec(memory_space=pltpu.VMEM)),
        scratch_shapes=[
            pltpu.VMEM(shape, jnp.float32),
            pltpu.VMEM((hops,) + shape, jnp.float32),
            pltpu.VMEM((heads, rows, lanes), jnp.bfloat16),
            pltpu.SemaphoreType.DMA((hops,)),
            pltpu.SemaphoreType.DMA((hops,)),
            pltpu.SemaphoreType.DMA((groups,)),
            pltpu.SemaphoreType.DMA((groups,)),
        ],
        compiler_params=pltpu.CompilerParams(collective_id=0, has_side_effects=True),
        cost_estimate=pl.CostEstimate(flops=0, transcendentals=0, bytes_accessed=512 * msg.size * 4),
    )(msg, after)
    return spread.reshape(groups * heads, rows, lanes)


def on_device(
    names,
    mixer_input, step_sizes, decay_rates, skip_gain, input_basis, output_basis, out_weight
):
    heads_here = step_sizes.shape[0]
    tokens_here = step_sizes.shape[1]
    count = tokens_here // GROUP
    channels = mixer_input.reshape(heads_here, HP, count, GROUP)
    log_decay = -(decay_rates[:, None] * step_sizes).reshape(heads_here, count, GROUP)
    steps_blocked = step_sizes.reshape(heads_here, count, GROUP)
    running = jnp.cumsum(log_decay, axis=2)
    basis_in_blocked = input_basis.reshape(count, GROUP, N)
    basis_out_blocked = output_basis.reshape(count, GROUP, N)
    gram = jnp.einsum(
        "cin,cjn->cij", basis_out_blocked, basis_in_blocked, preferred_element_type=jnp.float32
    )
    rows_index = lax.broadcasted_iota(jnp.int32, (GROUP, GROUP), 0)
    cols_index = lax.broadcasted_iota(jnp.int32, (GROUP, GROUP), 1)
    causal = rows_index >= cols_index
    gaps = running[:, :, :, None] - running[:, :, None, :]
    mixing = jnp.where(
        causal,
        gram[None] * jnp.exp(jnp.where(causal, gaps, 0.0)) * steps_blocked[:, :, None, :],
        0.0,
    ).astype(jnp.bfloat16)
    inner = jnp.einsum("hcij,hpcj->hpci", mixing, channels, preferred_element_type=jnp.float32)
    tail_decay = jnp.exp(running[:, :, -1:] - running) * steps_blocked
    weighted_terms = (basis_in_blocked.astype(jnp.float32)[None] * tail_decay[:, :, :, None]).astype(
        jnp.bfloat16
    )
    summaries = jnp.einsum(
        "hcjn,hpcj->chnp", weighted_terms, channels, preferred_element_type=jnp.float32
    )
    block_sums = jnp.sum(log_decay, axis=2)
    block_cum = jnp.cumsum(block_sums, axis=1)
    log_prefix = block_cum - block_sums
    total_log = block_cum[:, -1]
    entering = [jnp.zeros_like(summaries[0])]
    for c in range(1, count + 1):
        reach = log_prefix[:, c] if c < count else total_log
        term = jnp.zeros_like(summaries[0])
        for earlier in range(c):
            weight = jnp.exp(reach - block_cum[:, earlier])
            term = term + weight[:, None, None] * summaries[earlier]
        entering.append(term)
    final_state = entering[count]
    entering = jnp.stack(entering[:count])
    basis_out_wide = basis_out_blocked.astype(jnp.float32)
    within = jnp.exp(running)[:, None]
    direct = skip_gain[:, None, None, None] * channels.astype(jnp.float32)
    from_local = jnp.einsum(
        "cin,chnp->hpci", basis_out_wide, entering, precision=lax.Precision.HIGHEST
    )
    local = (inner + from_local * within + direct).astype(jnp.bfloat16)
    scale = jnp.exp(running + log_prefix[:, :, None]).reshape(heads_here, tokens_here)
    scale_hi = scale.astype(jnp.bfloat16)
    scale_lo = (scale - scale_hi.astype(jnp.float32)).astype(jnp.bfloat16)
    extra = 32 - 2 * heads_here
    local_ext = jnp.concatenate(
        [
            local.reshape(heads_here * HP, tokens_here),
            scale_hi,
            scale_lo,
            jnp.zeros((extra, tokens_here), jnp.bfloat16),
        ],
        axis=0,
    )
    local_all = lax.all_gather(local_ext, "grp", axis=0, tiled=True)
    carried_t = carry_in(total_log, jnp.swapaxes(final_state, 1, 2), names, local_ext)
    result_t = tail(local_all, output_basis, carried_t, out_weight.T)
    return result_t.T


def tail_kernel(local_ref, basis_ref, carried_ref, weight_ref, out_ref, acc_ref, mixed_ref):
    g = pl.program_id(0)

    @pl.when(g == 0)
    def _():
        acc_ref[...] = jnp.zeros_like(acc_ref)

    basis = basis_ref[...]
    per = carried_ref.shape[0]
    base = per * HP
    for h in range(per):
        rows = pl.ds(h * HP, HP)
        carry = lax.dot_general(
            carried_ref[h], basis, (((1,), (1,)), ((), ())), preferred_element_type=jnp.float32
        )
        mixed_ref[rows, :] = (
            local_ref[rows, :].astype(jnp.float32)
            + carry
            * (
                local_ref[pl.ds(base + h, 1), :].astype(jnp.float32)
                + local_ref[pl.ds(base + per + h, 1), :].astype(jnp.float32)
            )
        ).astype(jnp.bfloat16)
    acc_ref[...] += jnp.dot(weight_ref[...], mixed_ref[...], preferred_element_type=jnp.float32)

    @pl.when(g == pl.num_programs(0) - 1)
    def _():
        out_ref[...] = acc_ref[...].astype(out_ref.dtype)


def tail(local_all, basis, carried_t, weight_t):
    channels, tokens = local_all.shape
    features = weight_t.shape[0]
    heads = carried_t.shape[0]
    groups = lax.axis_size("grp")
    per = heads // groups
    return pl.pallas_call(
        tail_kernel,
        out_shape=jax.ShapeDtypeStruct((features, tokens), jnp.bfloat16),
        grid=(groups,),
        in_specs=[
            pl.BlockSpec((channels // groups, tokens), lambda g: (g, 0)),
            pl.BlockSpec(basis.shape, lambda g: (0, 0)),
            pl.BlockSpec((per, HP, N), lambda g: (g, 0, 0)),
            pl.BlockSpec((features, per * HP), lambda g: (0, g)),
        ],
        out_specs=pl.BlockSpec((features, tokens), lambda g: (0, 0)),
        scratch_shapes=[
            pltpu.VMEM((features, tokens), jnp.float32),
            pltpu.VMEM((per * HP, tokens), jnp.bfloat16),
        ],
        cost_estimate=pl.CostEstimate(
            flops=2 * tokens * per * HP * groups * (N + features),
            transcendentals=0,
            bytes_accessed=2 * (local_all.size + weight_t.size) + 2 * features * tokens,
        ),
    )(local_all, basis, carried_t, weight_t)


def solution(mesh):
    placed = (
        P("grp", "seq"),
        P("grp", "seq"),
        P("grp"),
        P("grp"),
        P("seq", None),
        P("seq", None),
        P(None, "grp"),
    )
    return jax.shard_map(
        functools.partial(on_device, mesh.axis_names), mesh=mesh, in_specs=placed, out_specs=P("seq", "grp"), check_vma=False
    )
```

```python
import functools

import jax
import jax.numpy as jnp
from jax import lax
from jax.experimental import pallas as pl
from jax.experimental.pallas import tpu as pltpu
from jax.sharding import PartitionSpec as P

HP = 64
N = 128
GROUP = 256


def scan_kernel(peers, names, msg_ref, after_ref, out_ref, spread_ref, inc_ref, recv_ref, send_ref,
                send_sem, recv_sem, spread_send, spread_recv):
    here = lax.axis_index("seq")
    grp_here = lax.axis_index("grp")
    groups = spread_ref.shape[0]
    rows = msg_ref.shape[0] - 8

    def device(seq_at, grp_at):
        return tuple(seq_at if name == "seq" else grp_at for name in names)

    offsets = sorted({d % peers for d in _hops(peers)} | {(-d) % peers for d in _hops(peers)})
    barrier = pltpu.get_barrier_semaphore()
    for offset in offsets:
        pl.semaphore_signal(
            barrier, inc=1, device_id=device(lax.rem(here + offset, peers), grp_here),
            device_id_type=pl.DeviceIdType.MESH,
        )
    for offset in range(1, groups):
        pl.semaphore_signal(
            barrier, inc=1, device_id=device(here, lax.rem(grp_here + offset, groups)),
            device_id_type=pl.DeviceIdType.MESH,
        )
    pl.semaphore_wait(barrier, len(offsets) + groups - 1)

    heads = rows // HP
    inc_ref[...] = msg_ref[...]
    out_ref[:rows] = jnp.zeros((rows, out_ref.shape[1]), jnp.float32)
    out_ref[rows:] = jnp.ones((8, out_ref.shape[1]), jnp.float32)
    for r, d in enumerate(_hops(peers)):
        copy = pltpu.make_async_remote_copy(
            src_ref=inc_ref,
            dst_ref=recv_ref.at[r],
            send_sem=send_sem.at[r],
            recv_sem=recv_sem.at[r],
            device_id=device(lax.rem(here + d, peers), grp_here),
            device_id_type=pl.DeviceIdType.MESH,
        )
        copy.start()
        copy.wait()
        reached = here >= d
        for ref in ((out_ref, inc_ref) if 2 * d < peers else (out_ref,)):
            decay = ref[rows:rows + 1, :]
            for h in range(heads):
                part = pl.ds(h * HP, HP)
                own = ref[part, :]
                ref[part, :] = jnp.where(reached, decay[:, h:h + 1] * recv_ref[r, part, :] + own, own)
            ref[rows:] = jnp.where(reached, ref[rows:] * recv_ref[r, rows:, :], ref[rows:])

    send_ref[...] = out_ref[:rows].astype(send_ref.dtype)
    spread_ref[grp_here] = out_ref[:rows].astype(spread_ref.dtype)
    copies = []
    for offset in range(1, groups):
        copy = pltpu.make_async_remote_copy(
            src_ref=send_ref,
            dst_ref=spread_ref.at[grp_here],
            send_sem=spread_send.at[offset],
            recv_sem=spread_recv.at[grp_here],
            device_id=device(here, lax.rem(grp_here + offset, groups)),
            device_id_type=pl.DeviceIdType.MESH,
        )
        copy.start()
        copies.append(copy)
    for copy in copies:
        copy.wait_send()
    for offset in range(1, groups):
        source = lax.rem(grp_here + groups - offset, groups)
        pltpu.make_async_remote_copy(
            src_ref=send_ref,
            dst_ref=spread_ref.at[source],
            send_sem=spread_send.at[offset],
            recv_sem=spread_recv.at[source],
            device_id=device(here, source),
            device_id_type=pl.DeviceIdType.MESH,
        ).wait_recv()


def _hops(peers):
    d, hops = 1, []
    while d < peers:
        hops.append(d)
        d *= 2
    return hops


def carry_in(total_log, state_t, names, after):
    peers = lax.axis_size("seq")
    groups = lax.axis_size("grp")
    heads, width, lanes = state_t.shape
    rows = heads * width
    decay = jnp.ones((8, lanes), jnp.float32).at[0, :heads].set(jnp.exp(total_log))
    msg = jnp.concatenate([state_t.reshape(rows, lanes), decay], axis=0)
    shape = msg.shape
    hops = len(_hops(peers))
    _, spread = pl.pallas_call(
        functools.partial(scan_kernel, peers, names),
        out_shape=(
            jax.ShapeDtypeStruct(shape, jnp.float32),
            jax.ShapeDtypeStruct((groups, rows, lanes), jnp.bfloat16),
        ),
        in_specs=[pl.BlockSpec(memory_space=pltpu.VMEM), pl.BlockSpec(memory_space=pl.ANY)],
        out_specs=(pl.BlockSpec(memory_space=pltpu.VMEM), pl.BlockSpec(memory_space=pltpu.VMEM)),
        scratch_shapes=[
            pltpu.VMEM(shape, jnp.float32),
            pltpu.VMEM((hops,) + shape, jnp.float32),
            pltpu.VMEM((rows, lanes), jnp.bfloat16),
            pltpu.SemaphoreType.DMA((hops,)),
            pltpu.SemaphoreType.DMA((hops,)),
            pltpu.SemaphoreType.DMA((groups,)),
            pltpu.SemaphoreType.DMA((groups,)),
        ],
        compiler_params=pltpu.CompilerParams(collective_id=0, has_side_effects=True),
        cost_estimate=pl.CostEstimate(flops=0, transcendentals=0, bytes_accessed=512 * msg.size * 4),
    )(msg, after)
    return spread.reshape(groups * rows, lanes)


def on_device(
    names,
    mixer_input, step_sizes, decay_rates, skip_gain, input_basis, output_basis, out_weight
):
    heads_here = step_sizes.shape[0]
    tokens_here = step_sizes.shape[1]
    count = tokens_here // GROUP
    channels = mixer_input.reshape(heads_here, HP, count, GROUP)
    log_decay = -(decay_rates[:, None] * step_sizes).reshape(heads_here, count, GROUP)
    steps_blocked = step_sizes.reshape(heads_here, count, GROUP)
    running = jnp.cumsum(log_decay, axis=2)
    basis_in_blocked = input_basis.reshape(count, GROUP, N)
    basis_out_blocked = output_basis.reshape(count, GROUP, N)
    gram = jnp.einsum(
        "cin,cjn->cij", basis_out_blocked, basis_in_blocked, preferred_element_type=jnp.float32
    )
    rows_index = lax.broadcasted_iota(jnp.int32, (GROUP, GROUP), 0)
    cols_index = lax.broadcasted_iota(jnp.int32, (GROUP, GROUP), 1)
    causal = rows_index >= cols_index
    gaps = running[:, :, :, None] - running[:, :, None, :]
    mixing = jnp.where(
        causal,
        gram[None] * jnp.exp(jnp.where(causal, gaps, 0.0)) * steps_blocked[:, :, None, :],
        0.0,
    ).astype(jnp.bfloat16)
    inner = jnp.einsum("hcij,hpcj->hpci", mixing, channels, preferred_element_type=jnp.float32)
    tail_decay = jnp.exp(running[:, :, -1:] - running) * steps_blocked
    weighted_terms = (basis_in_blocked.astype(jnp.float32)[None] * tail_decay[:, :, :, None]).astype(
        jnp.bfloat16
    )
    summaries = jnp.einsum(
        "hcjn,hpcj->chnp", weighted_terms, channels, preferred_element_type=jnp.float32
    )
    block_sums = jnp.sum(log_decay, axis=2)
    block_cum = jnp.cumsum(block_sums, axis=1)
    log_prefix = block_cum - block_sums
    total_log = block_cum[:, -1]
    entering = [jnp.zeros_like(summaries[0])]
    for c in range(1, count + 1):
        reach = log_prefix[:, c] if c < count else total_log
        term = jnp.zeros_like(summaries[0])
        for earlier in range(c):
            weight = jnp.exp(reach - block_cum[:, earlier])
            term = term + weight[:, None, None] * summaries[earlier]
        entering.append(term)
    final_state = entering[count]
    entering = jnp.stack(entering[:count])
    basis_out_wide = basis_out_blocked.astype(jnp.float32)
    within = jnp.exp(running)[:, None]
    direct = skip_gain[:, None, None, None] * channels.astype(jnp.float32)
    from_local = jnp.einsum(
        "cin,chnp->hpci", basis_out_wide, entering, precision=lax.Precision.HIGHEST
    )
    local = (inner + from_local * within + direct).astype(jnp.bfloat16)
    scale = jnp.exp(running + log_prefix[:, :, None]).reshape(heads_here, tokens_here)
    scale_hi = scale.astype(jnp.bfloat16)
    scale_lo = (scale - scale_hi.astype(jnp.float32)).astype(jnp.bfloat16)
    extra = 32 - 2 * heads_here
    local_ext = jnp.concatenate(
        [
            local.reshape(heads_here * HP, tokens_here),
            scale_hi,
            scale_lo,
            jnp.zeros((extra, tokens_here), jnp.bfloat16),
        ],
        axis=0,
    )
    local_all = lax.all_gather(local_ext, "grp", axis=0, tiled=True)
    carried_t = carry_in(total_log, jnp.swapaxes(final_state, 1, 2), names, local_ext)
    result_t = tail(local_all, output_basis, carried_t, out_weight.T)
    return result_t.T


def tail_kernel(local_ref, basis_ref, carried_ref, weight_ref, out_ref, acc_ref, mixed_ref):
    g = pl.program_id(0)

    @pl.when(g == 0)
    def _():
        acc_ref[...] = jnp.zeros_like(acc_ref)

    base, tokens = mixed_ref.shape
    per = base // HP
    carry = lax.dot_general(
        carried_ref[...], basis_ref[...], (((1,), (1,)), ((), ())), preferred_element_type=jnp.float32
    )
    scale = local_ref[pl.ds(base, per), :].astype(jnp.float32) + local_ref[
        pl.ds(base + per, per), :
    ].astype(jnp.float32)
    carry = (carry.reshape(per, HP, tokens) * scale[:, None, :]).reshape(base, tokens)
    mixed_ref[...] = (local_ref[pl.ds(0, base), :].astype(jnp.float32) + carry).astype(jnp.bfloat16)
    acc_ref[...] += jnp.dot(weight_ref[...], mixed_ref[...], preferred_element_type=jnp.float32)

    @pl.when(g == pl.num_programs(0) - 1)
    def _():
        out_ref[...] = acc_ref[...].astype(out_ref.dtype)


def tail(local_all, basis, carried_t, weight_t):
    channels, tokens = local_all.shape
    features = weight_t.shape[0]
    groups = lax.axis_size("grp")
    per = carried_t.shape[0] // groups // HP
    return pl.pallas_call(
        tail_kernel,
        out_shape=jax.ShapeDtypeStruct((features, tokens), jnp.bfloat16),
        grid=(groups,),
        in_specs=[
            pl.BlockSpec((channels // groups, tokens), lambda g: (g, 0)),
            pl.BlockSpec(basis.shape, lambda g: (0, 0)),
            pl.BlockSpec((per * HP, N), lambda g: (g, 0)),
            pl.BlockSpec((features, per * HP), lambda g: (0, g)),
        ],
        out_specs=pl.BlockSpec((features, tokens), lambda g: (0, 0)),
        scratch_shapes=[
            pltpu.VMEM((features, tokens), jnp.float32),
            pltpu.VMEM((per * HP, tokens), jnp.bfloat16),
        ],
        cost_estimate=pl.CostEstimate(
            flops=2 * tokens * per * HP * groups * (N + features),
            transcendentals=0,
            bytes_accessed=2 * (local_all.size + weight_t.size) + 2 * features * tokens,
        ),
    )(local_all, basis, carried_t, weight_t)


def solution(mesh):
    placed = (
        P("grp", "seq"),
        P("grp", "seq"),
        P("grp"),
        P("grp"),
        P("seq", None),
        P("seq", None),
        P(None, "grp"),
    )
    return jax.shard_map(
        functools.partial(on_device, mesh.axis_names), mesh=mesh, in_specs=placed, out_specs=P("seq", "grp"), check_vma=False
    )
```

```python
import functools

import jax
import jax.numpy as jnp
from jax import lax
from jax.experimental import pallas as pl
from jax.experimental.pallas import tpu as pltpu
from jax.sharding import PartitionSpec as P

HP = 64
N = 128
GROUP = 256


def scan_kernel(peers, names, msg_ref, after_ref, out_ref, spread_ref, inc_ref, out_state, recv_state,
                recv_decay, send_ref, send_sem, recv_sem, decay_send, decay_recv, spread_send, spread_recv):
    here = lax.axis_index("seq")
    grp_here = lax.axis_index("grp")
    groups = spread_ref.shape[0]
    rows = msg_ref.shape[0] - 8
    heads = rows // HP

    def device(seq_at, grp_at):
        return tuple(seq_at if name == "seq" else grp_at for name in names)

    offsets = sorted({d % peers for d in _hops(peers)} | {(-d) % peers for d in _hops(peers)})
    barrier = pltpu.get_barrier_semaphore()
    for offset in offsets:
        pl.semaphore_signal(
            barrier, inc=1, device_id=device(lax.rem(here + offset, peers), grp_here),
            device_id_type=pl.DeviceIdType.MESH,
        )
    for offset in range(1, groups):
        pl.semaphore_signal(
            barrier, inc=1, device_id=device(here, lax.rem(grp_here + offset, groups)),
            device_id_type=pl.DeviceIdType.MESH,
        )
    pl.semaphore_wait(barrier, len(offsets) + groups - 1)

    inc_ref[...] = msg_ref[...]
    out_ref[:rows] = jnp.zeros((rows, out_ref.shape[1]), jnp.float32)
    out_ref[rows:] = jnp.ones((8, out_ref.shape[1]), jnp.float32)
    for r, d in enumerate(_hops(peers)):
        target = device(lax.rem(here + d, peers), grp_here)
        out_state[r] = inc_ref[:rows].astype(out_state.dtype)
        state_copy = pltpu.make_async_remote_copy(
            src_ref=out_state.at[r],
            dst_ref=recv_state.at[r],
            send_sem=send_sem.at[r],
            recv_sem=recv_sem.at[r],
            device_id=target,
            device_id_type=pl.DeviceIdType.MESH,
        )
        decay_copy = pltpu.make_async_remote_copy(
            src_ref=inc_ref.at[pl.ds(rows, 8)],
            dst_ref=recv_decay.at[r],
            send_sem=decay_send.at[r],
            recv_sem=decay_recv.at[r],
            device_id=target,
            device_id_type=pl.DeviceIdType.MESH,
        )
        state_copy.start()
        decay_copy.start()
        state_copy.wait()
        decay_copy.wait()
        reached = here >= d
        for ref in ((out_ref, inc_ref) if 2 * d < peers else (out_ref,)):
            decay = ref[rows:rows + 1, :]
            for h in range(heads):
                part = pl.ds(h * HP, HP)
                own = ref[part, :]
                got = recv_state[r, part, :].astype(jnp.float32)
                ref[part, :] = jnp.where(reached, decay[:, h:h + 1] * got + own, own)
            ref[rows:] = jnp.where(reached, ref[rows:] * recv_decay[r], ref[rows:])

    send_ref[...] = out_ref[:rows].astype(send_ref.dtype)
    spread_ref[grp_here] = out_ref[:rows].astype(spread_ref.dtype)
    copies = []
    for offset in range(1, groups):
        copy = pltpu.make_async_remote_copy(
            src_ref=send_ref,
            dst_ref=spread_ref.at[grp_here],
            send_sem=spread_send.at[offset],
            recv_sem=spread_recv.at[grp_here],
            device_id=device(here, lax.rem(grp_here + offset, groups)),
            device_id_type=pl.DeviceIdType.MESH,
        )
        copy.start()
        copies.append(copy)
    for copy in copies:
        copy.wait_send()
    for offset in range(1, groups):
        source = lax.rem(grp_here + groups - offset, groups)
        pltpu.make_async_remote_copy(
            src_ref=send_ref,
            dst_ref=spread_ref.at[source],
            send_sem=spread_send.at[offset],
            recv_sem=spread_recv.at[source],
            device_id=device(here, source),
            device_id_type=pl.DeviceIdType.MESH,
        ).wait_recv()


def _hops(peers):
    d, hops = 1, []
    while d < peers:
        hops.append(d)
        d *= 2
    return hops


def carry_in(total_log, state_t, names, after):
    peers = lax.axis_size("seq")
    groups = lax.axis_size("grp")
    heads, width, lanes = state_t.shape
    rows = heads * width
    decay = jnp.ones((8, lanes), jnp.float32).at[0, :heads].set(jnp.exp(total_log))
    msg = jnp.concatenate([state_t.reshape(rows, lanes), decay], axis=0)
    shape = msg.shape
    hops = len(_hops(peers))
    _, spread = pl.pallas_call(
        functools.partial(scan_kernel, peers, names),
        out_shape=(
            jax.ShapeDtypeStruct(shape, jnp.float32),
            jax.ShapeDtypeStruct((groups, rows, lanes), jnp.bfloat16),
        ),
        in_specs=[pl.BlockSpec(memory_space=pltpu.VMEM), pl.BlockSpec(memory_space=pl.ANY)],
        out_specs=(pl.BlockSpec(memory_space=pltpu.VMEM), pl.BlockSpec(memory_space=pltpu.VMEM)),
        scratch_shapes=[
            pltpu.VMEM(shape, jnp.float32),
            pltpu.VMEM((hops, rows, lanes), jnp.bfloat16),
            pltpu.VMEM((hops, rows, lanes), jnp.bfloat16),
            pltpu.VMEM((hops, 8, lanes), jnp.float32),
            pltpu.VMEM((rows, lanes), jnp.bfloat16),
            pltpu.SemaphoreType.DMA((hops,)),
            pltpu.SemaphoreType.DMA((hops,)),
            pltpu.SemaphoreType.DMA((hops,)),
            pltpu.SemaphoreType.DMA((hops,)),
            pltpu.SemaphoreType.DMA((groups,)),
            pltpu.SemaphoreType.DMA((groups,)),
        ],
        compiler_params=pltpu.CompilerParams(collective_id=0, has_side_effects=True),
        cost_estimate=pl.CostEstimate(flops=0, transcendentals=0, bytes_accessed=512 * msg.size * 4),
    )(msg, after)
    return spread.reshape(groups * rows, lanes)


def on_device(
    names,
    mixer_input, step_sizes, decay_rates, skip_gain, input_basis, output_basis, out_weight
):
    heads_here = step_sizes.shape[0]
    tokens_here = step_sizes.shape[1]
    count = tokens_here // GROUP
    channels = mixer_input.reshape(heads_here, HP, count, GROUP)
    log_decay = -(decay_rates[:, None] * step_sizes).reshape(heads_here, count, GROUP)
    steps_blocked = step_sizes.reshape(heads_here, count, GROUP)
    running = jnp.cumsum(log_decay, axis=2)
    basis_in_blocked = input_basis.reshape(count, GROUP, N)
    basis_out_blocked = output_basis.reshape(count, GROUP, N)
    gram = jnp.einsum(
        "cin,cjn->cij", basis_out_blocked, basis_in_blocked, preferred_element_type=jnp.float32
    )
    rows_index = lax.broadcasted_iota(jnp.int32, (GROUP, GROUP), 0)
    cols_index = lax.broadcasted_iota(jnp.int32, (GROUP, GROUP), 1)
    causal = rows_index >= cols_index
    gaps = running[:, :, :, None] - running[:, :, None, :]
    mixing = jnp.where(
        causal,
        gram[None] * jnp.exp(jnp.where(causal, gaps, 0.0)) * steps_blocked[:, :, None, :],
        0.0,
    ).astype(jnp.bfloat16)
    inner = jnp.einsum("hcij,hpcj->hpci", mixing, channels, preferred_element_type=jnp.float32)
    tail_decay = jnp.exp(running[:, :, -1:] - running) * steps_blocked
    weighted_terms = (basis_in_blocked.astype(jnp.float32)[None] * tail_decay[:, :, :, None]).astype(
        jnp.bfloat16
    )
    summaries = jnp.einsum(
        "hcjn,hpcj->chnp", weighted_terms, channels, preferred_element_type=jnp.float32
    )
    block_sums = jnp.sum(log_decay, axis=2)
    block_cum = jnp.cumsum(block_sums, axis=1)
    log_prefix = block_cum - block_sums
    total_log = block_cum[:, -1]
    entering = [jnp.zeros_like(summaries[0])]
    for c in range(1, count + 1):
        reach = log_prefix[:, c] if c < count else total_log
        term = jnp.zeros_like(summaries[0])
        for earlier in range(c):
            weight = jnp.exp(reach - block_cum[:, earlier])
            term = term + weight[:, None, None] * summaries[earlier]
        entering.append(term)
    final_state = entering[count]
    entering = jnp.stack(entering[:count])
    basis_out_wide = basis_out_blocked.astype(jnp.float32)
    within = jnp.exp(running)[:, None]
    direct = skip_gain[:, None, None, None] * channels.astype(jnp.float32)
    from_local = jnp.einsum(
        "cin,chnp->hpci", basis_out_wide, entering, precision=lax.Precision.HIGHEST
    )
    local = (inner + from_local * within + direct).astype(jnp.bfloat16)
    scale = jnp.exp(running + log_prefix[:, :, None]).reshape(heads_here, tokens_here)
    scale_hi = scale.astype(jnp.bfloat16)
    scale_lo = (scale - scale_hi.astype(jnp.float32)).astype(jnp.bfloat16)
    extra = 32 - 2 * heads_here
    local_ext = jnp.concatenate(
        [
            local.reshape(heads_here * HP, tokens_here),
            scale_hi,
            scale_lo,
            jnp.zeros((extra, tokens_here), jnp.bfloat16),
        ],
        axis=0,
    )
    local_all = lax.all_gather(local_ext, "grp", axis=0, tiled=True)
    carried_t = carry_in(total_log, jnp.swapaxes(final_state, 1, 2), names, local_ext)
    result_t = tail(local_all, output_basis, carried_t, out_weight.T)
    return result_t.T


def tail_kernel(local_ref, basis_ref, carried_ref, weight_ref, out_ref, acc_ref, mixed_ref):
    g = pl.program_id(0)

    @pl.when(g == 0)
    def _():
        acc_ref[...] = jnp.zeros_like(acc_ref)

    base, tokens = mixed_ref.shape
    per = base // HP
    carry = lax.dot_general(
        carried_ref[...], basis_ref[...], (((1,), (1,)), ((), ())), preferred_element_type=jnp.float32
    )
    scale = local_ref[pl.ds(base, per), :].astype(jnp.float32) + local_ref[
        pl.ds(base + per, per), :
    ].astype(jnp.float32)
    carry = (carry.reshape(per, HP, tokens) * scale[:, None, :]).reshape(base, tokens)
    mixed_ref[...] = (local_ref[pl.ds(0, base), :].astype(jnp.float32) + carry).astype(jnp.bfloat16)
    acc_ref[...] += jnp.dot(weight_ref[...], mixed_ref[...], preferred_element_type=jnp.float32)

    @pl.when(g == pl.num_programs(0) - 1)
    def _():
        out_ref[...] = acc_ref[...].astype(out_ref.dtype)


def tail(local_all, basis, carried_t, weight_t):
    channels, tokens = local_all.shape
    features = weight_t.shape[0]
    groups = lax.axis_size("grp")
    per = carried_t.shape[0] // groups // HP
    return pl.pallas_call(
        tail_kernel,
        out_shape=jax.ShapeDtypeStruct((features, tokens), jnp.bfloat16),
        grid=(groups,),
        in_specs=[
            pl.BlockSpec((channels // groups, tokens), lambda g: (g, 0)),
            pl.BlockSpec(basis.shape, lambda g: (0, 0)),
            pl.BlockSpec((per * HP, N), lambda g: (g, 0)),
            pl.BlockSpec((features, per * HP), lambda g: (0, g)),
        ],
        out_specs=pl.BlockSpec((features, tokens), lambda g: (0, 0)),
        scratch_shapes=[
            pltpu.VMEM((features, tokens), jnp.float32),
            pltpu.VMEM((per * HP, tokens), jnp.bfloat16),
        ],
        cost_estimate=pl.CostEstimate(
            flops=2 * tokens * per * HP * groups * (N + features),
            transcendentals=0,
            bytes_accessed=2 * (local_all.size + weight_t.size) + 2 * features * tokens,
        ),
    )(local_all, basis, carried_t, weight_t)


def solution(mesh):
    placed = (
        P("grp", "seq"),
        P("grp", "seq"),
        P("grp"),
        P("grp"),
        P("seq", None),
        P("seq", None),
        P(None, "grp"),
    )
    return jax.shard_map(
        functools.partial(on_device, mesh.axis_names), mesh=mesh, in_specs=placed, out_specs=P("seq", "grp"), check_vma=False
    )
```

```python
import functools

import jax
import jax.numpy as jnp
from jax import lax
from jax.experimental import pallas as pl
from jax.experimental.pallas import tpu as pltpu
from jax.sharding import PartitionSpec as P

HP = 64
N = 128
GROUP = 256


def scan_kernel(peers, names, msg_ref, local_ref, out_ref, spread_ref, gathered_ref, inc_ref, out_state,
                recv_state, recv_decay, send_ref, send_sem, recv_sem, decay_send, decay_recv, spread_send,
                spread_recv, ring_send, ring_recv, own_sem):
    here = lax.axis_index("seq")
    grp_here = lax.axis_index("grp")
    groups = spread_ref.shape[0]
    rows = msg_ref.shape[0] - 8
    heads = rows // HP

    def device(seq_at, grp_at):
        return tuple(seq_at if name == "seq" else grp_at for name in names)

    offsets = sorted({d % peers for d in _hops(peers)} | {(-d) % peers for d in _hops(peers)})
    barrier = pltpu.get_barrier_semaphore()
    for offset in offsets:
        pl.semaphore_signal(
            barrier, inc=1, device_id=device(lax.rem(here + offset, peers), grp_here),
            device_id_type=pl.DeviceIdType.MESH,
        )
    for offset in range(1, groups):
        pl.semaphore_signal(
            barrier, inc=1, device_id=device(here, lax.rem(grp_here + offset, groups)),
            device_id_type=pl.DeviceIdType.MESH,
        )
    pl.semaphore_wait(barrier, len(offsets) + groups - 1)

    inc_ref[...] = msg_ref[...]
    out_ref[:rows] = jnp.zeros((rows, out_ref.shape[1]), jnp.float32)
    out_ref[rows:] = jnp.ones((8, out_ref.shape[1]), jnp.float32)
    half = local_ref.shape[0] // 2
    right = device(here, lax.rem(grp_here + 1, groups))
    left = device(here, lax.rem(grp_here + groups - 1, groups))
    own_copy = pltpu.make_async_copy(local_ref, gathered_ref.at[grp_here], own_sem.at[0])
    own_copy.start()

    def ring(k, direction):
        first = pl.ds(0, half) if direction == 0 else pl.ds(half, half)
        if direction == 0:
            slot = lax.rem(grp_here + groups - k, groups)
        else:
            slot = lax.rem(grp_here + k, groups)
        source = local_ref.at[first] if k == 0 else gathered_ref.at[slot, first]
        return pltpu.make_async_remote_copy(
            src_ref=source,
            dst_ref=gathered_ref.at[slot, first],
            send_sem=ring_send.at[direction, k],
            recv_sem=ring_recv.at[direction, k],
            device_id=right if direction == 0 else left,
            device_id_type=pl.DeviceIdType.MESH,
        )

    def incoming(k, direction):
        first = pl.ds(0, half) if direction == 0 else pl.ds(half, half)
        if direction == 0:
            slot = lax.rem(grp_here + groups - 1 - k, groups)
        else:
            slot = lax.rem(grp_here + 1 + k, groups)
        return pltpu.make_async_remote_copy(
            src_ref=local_ref.at[first],
            dst_ref=gathered_ref.at[slot, first],
            send_sem=ring_send.at[direction, k],
            recv_sem=ring_recv.at[direction, k],
            device_id=left if direction == 0 else right,
            device_id_type=pl.DeviceIdType.MESH,
        )

    sent = []
    hops = _hops(peers)
    for k in range(max(groups - 1, len(hops))):
        if k < groups - 1:
            if k >= 1:
                incoming(k - 1, 0).wait_recv()
                incoming(k - 1, 1).wait_recv()
            for direction in (0, 1):
                copy = ring(k, direction)
                copy.start()
                sent.append(copy)
        if k < len(hops):
            r, d = k, hops[k]
            target = device(lax.rem(here + d, peers), grp_here)
            out_state[r] = inc_ref[:rows].astype(out_state.dtype)
            state_copy = pltpu.make_async_remote_copy(
                src_ref=out_state.at[r],
                dst_ref=recv_state.at[r],
                send_sem=send_sem.at[r],
                recv_sem=recv_sem.at[r],
                device_id=target,
                device_id_type=pl.DeviceIdType.MESH,
            )
            decay_copy = pltpu.make_async_remote_copy(
                src_ref=inc_ref.at[pl.ds(rows, 8)],
                dst_ref=recv_decay.at[r],
                send_sem=decay_send.at[r],
                recv_sem=decay_recv.at[r],
                device_id=target,
                device_id_type=pl.DeviceIdType.MESH,
            )
            state_copy.start()
            decay_copy.start()
            state_copy.wait()
            decay_copy.wait()
            reached = here >= d
            for ref in ((out_ref, inc_ref) if 2 * d < peers else (out_ref,)):
                decay = ref[rows:rows + 1, :]
                for h in range(heads):
                    part = pl.ds(h * HP, HP)
                    own = ref[part, :]
                    got = recv_state[r, part, :].astype(jnp.float32)
                    ref[part, :] = jnp.where(reached, decay[:, h:h + 1] * got + own, own)
                ref[rows:] = jnp.where(reached, ref[rows:] * recv_decay[r], ref[rows:])


    if groups > 1:
        incoming(groups - 2, 0).wait_recv()
        incoming(groups - 2, 1).wait_recv()
    for copy in sent:
        copy.wait_send()
    own_copy.wait()

    send_ref[...] = out_ref[:rows].astype(send_ref.dtype)
    spread_ref[grp_here] = out_ref[:rows].astype(spread_ref.dtype)
    copies = []
    for offset in range(1, groups):
        copy = pltpu.make_async_remote_copy(
            src_ref=send_ref,
            dst_ref=spread_ref.at[grp_here],
            send_sem=spread_send.at[offset],
            recv_sem=spread_recv.at[grp_here],
            device_id=device(here, lax.rem(grp_here + offset, groups)),
            device_id_type=pl.DeviceIdType.MESH,
        )
        copy.start()
        copies.append(copy)
    for copy in copies:
        copy.wait_send()
    for offset in range(1, groups):
        source = lax.rem(grp_here + groups - offset, groups)
        pltpu.make_async_remote_copy(
            src_ref=send_ref,
            dst_ref=spread_ref.at[source],
            send_sem=spread_send.at[offset],
            recv_sem=spread_recv.at[source],
            device_id=device(here, source),
            device_id_type=pl.DeviceIdType.MESH,
        ).wait_recv()


def _hops(peers):
    d, hops = 1, []
    while d < peers:
        hops.append(d)
        d *= 2
    return hops


def carry_in(total_log, state_t, names, local_ext):
    peers = lax.axis_size("seq")
    groups = lax.axis_size("grp")
    heads, width, lanes = state_t.shape
    rows = heads * width
    decay = jnp.ones((8, lanes), jnp.float32).at[0, :heads].set(jnp.exp(total_log))
    msg = jnp.concatenate([state_t.reshape(rows, lanes), decay], axis=0)
    shape = msg.shape
    hops = len(_hops(peers))
    _, spread, gathered = pl.pallas_call(
        functools.partial(scan_kernel, peers, names),
        out_shape=(
            jax.ShapeDtypeStruct(shape, jnp.float32),
            jax.ShapeDtypeStruct((groups, rows, lanes), jnp.bfloat16),
            jax.ShapeDtypeStruct((groups,) + local_ext.shape, jnp.bfloat16),
        ),
        in_specs=[pl.BlockSpec(memory_space=pltpu.VMEM), pl.BlockSpec(memory_space=pltpu.VMEM)],
        out_specs=(
            pl.BlockSpec(memory_space=pltpu.VMEM),
            pl.BlockSpec(memory_space=pltpu.VMEM),
            pl.BlockSpec(memory_space=pl.ANY),
        ),
        scratch_shapes=[
            pltpu.VMEM(shape, jnp.float32),
            pltpu.VMEM((hops, rows, lanes), jnp.bfloat16),
            pltpu.VMEM((hops, rows, lanes), jnp.bfloat16),
            pltpu.VMEM((hops, 8, lanes), jnp.float32),
            pltpu.VMEM((rows, lanes), jnp.bfloat16),
            pltpu.SemaphoreType.DMA((hops,)),
            pltpu.SemaphoreType.DMA((hops,)),
            pltpu.SemaphoreType.DMA((hops,)),
            pltpu.SemaphoreType.DMA((hops,)),
            pltpu.SemaphoreType.DMA((groups,)),
            pltpu.SemaphoreType.DMA((groups,)),
            pltpu.SemaphoreType.DMA((2, max(groups - 1, 1))),
            pltpu.SemaphoreType.DMA((2, max(groups - 1, 1))),
            pltpu.SemaphoreType.DMA((1,)),
        ],
        compiler_params=pltpu.CompilerParams(collective_id=0, has_side_effects=True),
        cost_estimate=pl.CostEstimate(flops=0, transcendentals=0, bytes_accessed=512 * msg.size * 4),
    )(msg, local_ext)
    return spread.reshape(groups * rows, lanes), gathered.reshape(groups * local_ext.shape[0], -1)


def on_device(
    names,
    mixer_input, step_sizes, decay_rates, skip_gain, input_basis, output_basis, out_weight
):
    heads_here = step_sizes.shape[0]
    tokens_here = step_sizes.shape[1]
    count = tokens_here // GROUP
    channels = mixer_input.reshape(heads_here, HP, count, GROUP)
    log_decay = -(decay_rates[:, None] * step_sizes).reshape(heads_here, count, GROUP)
    steps_blocked = step_sizes.reshape(heads_here, count, GROUP)
    running = jnp.cumsum(log_decay, axis=2)
    basis_in_blocked = input_basis.reshape(count, GROUP, N)
    basis_out_blocked = output_basis.reshape(count, GROUP, N)
    gram = jnp.einsum(
        "cin,cjn->cij", basis_out_blocked, basis_in_blocked, preferred_element_type=jnp.float32
    )
    rows_index = lax.broadcasted_iota(jnp.int32, (GROUP, GROUP), 0)
    cols_index = lax.broadcasted_iota(jnp.int32, (GROUP, GROUP), 1)
    causal = rows_index >= cols_index
    gaps = running[:, :, :, None] - running[:, :, None, :]
    mixing = jnp.where(
        causal,
        gram[None] * jnp.exp(jnp.where(causal, gaps, 0.0)) * steps_blocked[:, :, None, :],
        0.0,
    ).astype(jnp.bfloat16)
    inner = jnp.einsum("hcij,hpcj->hpci", mixing, channels, preferred_element_type=jnp.float32)
    tail_decay = jnp.exp(running[:, :, -1:] - running) * steps_blocked
    weighted_terms = (basis_in_blocked.astype(jnp.float32)[None] * tail_decay[:, :, :, None]).astype(
        jnp.bfloat16
    )
    summaries = jnp.einsum(
        "hcjn,hpcj->chnp", weighted_terms, channels, preferred_element_type=jnp.float32
    )
    block_sums = jnp.sum(log_decay, axis=2)
    block_cum = jnp.cumsum(block_sums, axis=1)
    log_prefix = block_cum - block_sums
    total_log = block_cum[:, -1]
    entering = [jnp.zeros_like(summaries[0])]
    for c in range(1, count + 1):
        reach = log_prefix[:, c] if c < count else total_log
        term = jnp.zeros_like(summaries[0])
        for earlier in range(c):
            weight = jnp.exp(reach - block_cum[:, earlier])
            term = term + weight[:, None, None] * summaries[earlier]
        entering.append(term)
    final_state = entering[count]
    entering = jnp.stack(entering[:count])
    basis_out_wide = basis_out_blocked.astype(jnp.float32)
    within = jnp.exp(running)[:, None]
    direct = skip_gain[:, None, None, None] * channels.astype(jnp.float32)
    from_local = jnp.einsum(
        "cin,chnp->hpci", basis_out_wide, entering, precision=lax.Precision.HIGHEST
    )
    local = (inner + from_local * within + direct).astype(jnp.bfloat16)
    scale = jnp.exp(running + log_prefix[:, :, None]).reshape(heads_here, tokens_here)
    scale_hi = scale.astype(jnp.bfloat16)
    scale_lo = (scale - scale_hi.astype(jnp.float32)).astype(jnp.bfloat16)
    extra = 32 - 2 * heads_here
    local_ext = jnp.concatenate(
        [
            local.reshape(heads_here * HP, tokens_here),
            scale_hi,
            scale_lo,
            jnp.zeros((extra, tokens_here), jnp.bfloat16),
        ],
        axis=0,
    )
    carried_t, local_all = carry_in(total_log, jnp.swapaxes(final_state, 1, 2), names, local_ext)
    result_t = tail(local_all, output_basis, carried_t, out_weight.T)
    return result_t.T


def tail_kernel(local_ref, basis_ref, carried_ref, weight_ref, out_ref, acc_ref, mixed_ref):
    g = pl.program_id(0)

    @pl.when(g == 0)
    def _():
        acc_ref[...] = jnp.zeros_like(acc_ref)

    base, tokens = mixed_ref.shape
    per = base // HP
    carry = lax.dot_general(
        carried_ref[...], basis_ref[...], (((1,), (1,)), ((), ())), preferred_element_type=jnp.float32
    )
    scale = local_ref[pl.ds(base, per), :].astype(jnp.float32) + local_ref[
        pl.ds(base + per, per), :
    ].astype(jnp.float32)
    carry = (carry.reshape(per, HP, tokens) * scale[:, None, :]).reshape(base, tokens)
    mixed_ref[...] = (local_ref[pl.ds(0, base), :].astype(jnp.float32) + carry).astype(jnp.bfloat16)
    acc_ref[...] += jnp.dot(weight_ref[...], mixed_ref[...], preferred_element_type=jnp.float32)

    @pl.when(g == pl.num_programs(0) - 1)
    def _():
        out_ref[...] = acc_ref[...].astype(out_ref.dtype)


def tail(local_all, basis, carried_t, weight_t):
    channels, tokens = local_all.shape
    features = weight_t.shape[0]
    groups = lax.axis_size("grp")
    per = carried_t.shape[0] // groups // HP
    return pl.pallas_call(
        tail_kernel,
        out_shape=jax.ShapeDtypeStruct((features, tokens), jnp.bfloat16),
        grid=(groups,),
        in_specs=[
            pl.BlockSpec((channels // groups, tokens), lambda g: (g, 0)),
            pl.BlockSpec(basis.shape, lambda g: (0, 0)),
            pl.BlockSpec((per * HP, N), lambda g: (g, 0)),
            pl.BlockSpec((features, per * HP), lambda g: (0, g)),
        ],
        out_specs=pl.BlockSpec((features, tokens), lambda g: (0, 0)),
        scratch_shapes=[
            pltpu.VMEM((features, tokens), jnp.float32),
            pltpu.VMEM((per * HP, tokens), jnp.bfloat16),
        ],
        cost_estimate=pl.CostEstimate(
            flops=2 * tokens * per * HP * groups * (N + features),
            transcendentals=0,
            bytes_accessed=2 * (local_all.size + weight_t.size) + 2 * features * tokens,
        ),
    )(local_all, basis, carried_t, weight_t)


def solution(mesh):
    placed = (
        P("grp", "seq"),
        P("grp", "seq"),
        P("grp"),
        P("grp"),
        P("seq", None),
        P("seq", None),
        P(None, "grp"),
    )
    return jax.shard_map(
        functools.partial(on_device, mesh.axis_names), mesh=mesh, in_specs=placed, out_specs=P("seq", "grp"), check_vma=False
    )
```

```python
import functools

import jax
import jax.numpy as jnp
from jax import lax
from jax.experimental import pallas as pl
from jax.experimental.pallas import tpu as pltpu
from jax.sharding import PartitionSpec as P

HP = 64
N = 128
GROUP = 256


def scan_kernel(peers, names, msg_ref, after_ref, out_ref, spread_ref, inc_ref, out_state, recv_state,
                recv_decay, send_ref, send_sem, recv_sem, decay_send, decay_recv, spread_send, spread_recv):
    here = lax.axis_index("seq")
    grp_here = lax.axis_index("grp")
    groups = spread_ref.shape[0]
    rows = msg_ref.shape[0] - 8
    heads = rows // HP

    def device(seq_at, grp_at):
        return tuple(seq_at if name == "seq" else grp_at for name in names)

    offsets = sorted({d % peers for d in _hops(peers)} | {(-d) % peers for d in _hops(peers)})
    barrier = pltpu.get_barrier_semaphore()
    for offset in offsets:
        pl.semaphore_signal(
            barrier, inc=1, device_id=device(lax.rem(here + offset, peers), grp_here),
            device_id_type=pl.DeviceIdType.MESH,
        )
    for offset in range(1, groups):
        pl.semaphore_signal(
            barrier, inc=1, device_id=device(here, lax.rem(grp_here + offset, groups)),
            device_id_type=pl.DeviceIdType.MESH,
        )
    pl.semaphore_wait(barrier, len(offsets) + groups - 1)

    inc_ref[...] = msg_ref[...]
    out_ref[:rows] = jnp.zeros((rows, out_ref.shape[1]), jnp.float32)
    out_ref[rows:] = jnp.ones((8, out_ref.shape[1]), jnp.float32)
    for r, d in enumerate(_hops(peers)):
        target = device(lax.rem(here + d, peers), grp_here)
        out_state[r] = inc_ref[:rows].astype(out_state.dtype)
        state_copy = pltpu.make_async_remote_copy(
            src_ref=out_state.at[r],
            dst_ref=recv_state.at[r],
            send_sem=send_sem.at[r],
            recv_sem=recv_sem.at[r],
            device_id=target,
            device_id_type=pl.DeviceIdType.MESH,
        )
        decay_copy = pltpu.make_async_remote_copy(
            src_ref=inc_ref.at[pl.ds(rows, 8)],
            dst_ref=recv_decay.at[r],
            send_sem=decay_send.at[r],
            recv_sem=decay_recv.at[r],
            device_id=target,
            device_id_type=pl.DeviceIdType.MESH,
        )
        state_copy.start()
        decay_copy.start()
        state_copy.wait()
        decay_copy.wait()
        reached = here >= d
        for ref in ((out_ref, inc_ref) if 2 * d < peers else (out_ref,)):
            decay = ref[rows:rows + 1, :]
            for h in range(heads):
                part = pl.ds(h * HP, HP)
                own = ref[part, :]
                got = recv_state[r, part, :].astype(jnp.float32)
                ref[part, :] = jnp.where(reached, decay[:, h:h + 1] * got + own, own)
            ref[rows:] = jnp.where(reached, ref[rows:] * recv_decay[r], ref[rows:])

    send_ref[...] = out_ref[:rows].astype(send_ref.dtype)
    spread_ref[grp_here] = out_ref[:rows].astype(spread_ref.dtype)
    copies = []
    for offset in range(1, groups):
        copy = pltpu.make_async_remote_copy(
            src_ref=send_ref,
            dst_ref=spread_ref.at[grp_here],
            send_sem=spread_send.at[offset],
            recv_sem=spread_recv.at[grp_here],
            device_id=device(here, lax.rem(grp_here + offset, groups)),
            device_id_type=pl.DeviceIdType.MESH,
        )
        copy.start()
        copies.append(copy)
    for copy in copies:
        copy.wait_send()
    for offset in range(1, groups):
        source = lax.rem(grp_here + groups - offset, groups)
        pltpu.make_async_remote_copy(
            src_ref=send_ref,
            dst_ref=spread_ref.at[source],
            send_sem=spread_send.at[offset],
            recv_sem=spread_recv.at[source],
            device_id=device(here, source),
            device_id_type=pl.DeviceIdType.MESH,
        ).wait_recv()


def _hops(peers):
    d, hops = 1, []
    while d < peers:
        hops.append(d)
        d *= 2
    return hops


def carry_in(total_log, state_t, names, after):
    peers = lax.axis_size("seq")
    groups = lax.axis_size("grp")
    heads, width, lanes = state_t.shape
    rows = heads * width
    decay = jnp.ones((8, lanes), jnp.float32).at[0, :heads].set(jnp.exp(total_log))
    msg = jnp.concatenate([state_t.reshape(rows, lanes), decay], axis=0)
    shape = msg.shape
    hops = len(_hops(peers))
    _, spread = pl.pallas_call(
        functools.partial(scan_kernel, peers, names),
        out_shape=(
            jax.ShapeDtypeStruct(shape, jnp.float32),
            jax.ShapeDtypeStruct((groups, rows, lanes), jnp.bfloat16),
        ),
        in_specs=[pl.BlockSpec(memory_space=pltpu.VMEM), pl.BlockSpec(memory_space=pl.ANY)],
        out_specs=(pl.BlockSpec(memory_space=pltpu.VMEM), pl.BlockSpec(memory_space=pltpu.VMEM)),
        scratch_shapes=[
            pltpu.VMEM(shape, jnp.float32),
            pltpu.VMEM((hops, rows, lanes), jnp.bfloat16),
            pltpu.VMEM((hops, rows, lanes), jnp.bfloat16),
            pltpu.VMEM((hops, 8, lanes), jnp.float32),
            pltpu.VMEM((rows, lanes), jnp.bfloat16),
            pltpu.SemaphoreType.DMA((hops,)),
            pltpu.SemaphoreType.DMA((hops,)),
            pltpu.SemaphoreType.DMA((hops,)),
            pltpu.SemaphoreType.DMA((hops,)),
            pltpu.SemaphoreType.DMA((groups,)),
            pltpu.SemaphoreType.DMA((groups,)),
        ],
        compiler_params=pltpu.CompilerParams(collective_id=0, has_side_effects=True),
        cost_estimate=pl.CostEstimate(flops=0, transcendentals=0, bytes_accessed=512 * msg.size * 4),
    )(msg, after)
    return spread.reshape(groups * rows, lanes)


def on_device(
    names,
    mixer_input, step_sizes, decay_rates, skip_gain, input_basis, output_basis, out_weight
):
    heads_here = step_sizes.shape[0]
    tokens_here = step_sizes.shape[1]
    count = tokens_here // GROUP
    channels = mixer_input.reshape(heads_here, HP, tokens_here)
    blocks = [channels[:, :, c * GROUP : (c + 1) * GROUP] for c in range(count)]
    log_decay = -(decay_rates[:, None] * step_sizes).reshape(heads_here, count, GROUP)
    steps_blocked = step_sizes.reshape(heads_here, count, GROUP)
    running = jnp.cumsum(log_decay, axis=2)
    basis_in_blocked = input_basis.reshape(count, GROUP, N)
    basis_out_blocked = output_basis.reshape(count, GROUP, N)
    gram = jnp.einsum(
        "cin,cjn->cij", basis_out_blocked, basis_in_blocked, preferred_element_type=jnp.float32
    )
    rows_index = lax.broadcasted_iota(jnp.int32, (GROUP, GROUP), 0)
    cols_index = lax.broadcasted_iota(jnp.int32, (GROUP, GROUP), 1)
    causal = rows_index >= cols_index
    gaps = running[:, :, :, None] - running[:, :, None, :]
    mixing = jnp.where(
        causal,
        gram[None] * jnp.exp(jnp.where(causal, gaps, 0.0)) * steps_blocked[:, :, None, :],
        0.0,
    ).astype(jnp.bfloat16)
    tail_decay = jnp.exp(running[:, :, -1:] - running) * steps_blocked
    weighted_terms = (basis_in_blocked.astype(jnp.float32)[None] * tail_decay[:, :, :, None]).astype(
        jnp.bfloat16
    )
    summaries = [
        jnp.einsum(
            "hjn,hpj->hnp", weighted_terms[:, c], blocks[c], preferred_element_type=jnp.float32
        )
        for c in range(count)
    ]
    block_sums = jnp.sum(log_decay, axis=2)
    block_cum = jnp.cumsum(block_sums, axis=1)
    log_prefix = block_cum - block_sums
    total_log = block_cum[:, -1]
    entering = [jnp.zeros_like(summaries[0])]
    for c in range(1, count + 1):
        reach = log_prefix[:, c] if c < count else total_log
        term = jnp.zeros_like(summaries[0])
        for earlier in range(c):
            weight = jnp.exp(reach - block_cum[:, earlier])
            term = term + weight[:, None, None] * summaries[earlier]
        entering.append(term)
    final_state = entering[count]
    within = jnp.exp(running)
    pieces = []
    for c in range(count):
        inner = jnp.einsum(
            "hij,hpj->hpi", mixing[:, c], blocks[c], preferred_element_type=jnp.float32
        )
        from_local = jnp.einsum(
            "in,hnp->hpi",
            basis_out_blocked[c].astype(jnp.float32),
            entering[c],
            precision=lax.Precision.HIGHEST,
        )
        direct = skip_gain[:, None, None] * blocks[c].astype(jnp.float32)
        pieces.append(inner + from_local * within[:, c][:, None, :] + direct)
    local = jnp.concatenate(pieces, axis=2).astype(jnp.bfloat16)
    scale = jnp.exp(running + log_prefix[:, :, None]).reshape(heads_here, tokens_here)
    scale_hi = scale.astype(jnp.bfloat16)
    scale_lo = (scale - scale_hi.astype(jnp.float32)).astype(jnp.bfloat16)
    extra = 32 - 2 * heads_here
    local_ext = jnp.concatenate(
        [
            local.reshape(heads_here * HP, tokens_here),
            scale_hi,
            scale_lo,
            jnp.zeros((extra, tokens_here), jnp.bfloat16),
        ],
        axis=0,
    )
    local_all = lax.all_gather(local_ext, "grp", axis=0, tiled=True)
    carried_t = carry_in(total_log, jnp.swapaxes(final_state, 1, 2), names, local_ext)
    result_t = tail(local_all, output_basis, carried_t, out_weight.T)
    return result_t.T


def tail_kernel(local_ref, basis_ref, carried_ref, weight_ref, out_ref, acc_ref, mixed_ref):
    g = pl.program_id(0)

    @pl.when(g == 0)
    def _():
        acc_ref[...] = jnp.zeros_like(acc_ref)

    base, tokens = mixed_ref.shape
    per = base // HP
    carry = lax.dot_general(
        carried_ref[...], basis_ref[...], (((1,), (1,)), ((), ())), preferred_element_type=jnp.float32
    )
    scale = local_ref[pl.ds(base, per), :].astype(jnp.float32) + local_ref[
        pl.ds(base + per, per), :
    ].astype(jnp.float32)
    carry = (carry.reshape(per, HP, tokens) * scale[:, None, :]).reshape(base, tokens)
    mixed_ref[...] = (local_ref[pl.ds(0, base), :].astype(jnp.float32) + carry).astype(jnp.bfloat16)
    acc_ref[...] += jnp.dot(weight_ref[...], mixed_ref[...], preferred_element_type=jnp.float32)

    @pl.when(g == pl.num_programs(0) - 1)
    def _():
        out_ref[...] = acc_ref[...].astype(out_ref.dtype)


def tail(local_all, basis, carried_t, weight_t):
    channels, tokens = local_all.shape
    features = weight_t.shape[0]
    groups = lax.axis_size("grp")
    per = carried_t.shape[0] // groups // HP
    return pl.pallas_call(
        tail_kernel,
        out_shape=jax.ShapeDtypeStruct((features, tokens), jnp.bfloat16),
        grid=(groups,),
        in_specs=[
            pl.BlockSpec((channels // groups, tokens), lambda g: (g, 0)),
            pl.BlockSpec(basis.shape, lambda g: (0, 0)),
            pl.BlockSpec((per * HP, N), lambda g: (g, 0)),
            pl.BlockSpec((features, per * HP), lambda g: (0, g)),
        ],
        out_specs=pl.BlockSpec((features, tokens), lambda g: (0, 0)),
        scratch_shapes=[
            pltpu.VMEM((features, tokens), jnp.float32),
            pltpu.VMEM((per * HP, tokens), jnp.bfloat16),
        ],
        cost_estimate=pl.CostEstimate(
            flops=2 * tokens * per * HP * groups * (N + features),
            transcendentals=0,
            bytes_accessed=2 * (local_all.size + weight_t.size) + 2 * features * tokens,
        ),
    )(local_all, basis, carried_t, weight_t)


def solution(mesh):
    placed = (
        P("grp", "seq"),
        P("grp", "seq"),
        P("grp"),
        P("grp"),
        P("seq", None),
        P("seq", None),
        P(None, "grp"),
    )
    return jax.shard_map(
        functools.partial(on_device, mesh.axis_names), mesh=mesh, in_specs=placed, out_specs=P("seq", "grp"), check_vma=False
    )
```

```python
import functools

import jax
import jax.numpy as jnp
from jax import lax
from jax.experimental import pallas as pl
from jax.experimental.pallas import tpu as pltpu
from jax.sharding import PartitionSpec as P

HP = 64
N = 128
GROUP = 256


def scan_kernel(peers, names, msg_ref, after_ref, scale_ref, out_ref, spread_ref, inc_ref, out_state, recv_state,
                recv_decay, send_ref, send_sem, recv_sem, decay_send, decay_recv, spread_send, spread_recv):
    here = lax.axis_index("seq")
    grp_here = lax.axis_index("grp")
    groups = spread_ref.shape[0]
    rows = msg_ref.shape[0] - 8
    heads = rows // HP

    def device(seq_at, grp_at):
        return tuple(seq_at if name == "seq" else grp_at for name in names)

    offsets = sorted({d % peers for d in _hops(peers)} | {(-d) % peers for d in _hops(peers)})
    barrier = pltpu.get_barrier_semaphore()
    for offset in offsets:
        pl.semaphore_signal(
            barrier, inc=1, device_id=device(lax.rem(here + offset, peers), grp_here),
            device_id_type=pl.DeviceIdType.MESH,
        )
    for offset in range(1, groups):
        pl.semaphore_signal(
            barrier, inc=1, device_id=device(here, lax.rem(grp_here + offset, groups)),
            device_id_type=pl.DeviceIdType.MESH,
        )
    pl.semaphore_wait(barrier, len(offsets) + groups - 1)

    inc_ref[...] = msg_ref[...]
    out_ref[:rows] = jnp.zeros((rows, out_ref.shape[1]), jnp.float32)
    out_ref[rows:] = jnp.ones((8, out_ref.shape[1]), jnp.float32)
    for r, d in enumerate(_hops(peers)):
        target = device(lax.rem(here + d, peers), grp_here)
        out_state[r] = inc_ref[:rows].astype(out_state.dtype)
        state_copy = pltpu.make_async_remote_copy(
            src_ref=out_state.at[r],
            dst_ref=recv_state.at[r],
            send_sem=send_sem.at[r],
            recv_sem=recv_sem.at[r],
            device_id=target,
            device_id_type=pl.DeviceIdType.MESH,
        )
        decay_copy = pltpu.make_async_remote_copy(
            src_ref=inc_ref.at[pl.ds(rows, 8)],
            dst_ref=recv_decay.at[r],
            send_sem=decay_send.at[r],
            recv_sem=decay_recv.at[r],
            device_id=target,
            device_id_type=pl.DeviceIdType.MESH,
        )
        state_copy.start()
        decay_copy.start()
        state_copy.wait()
        decay_copy.wait()
        reached = here >= d
        for ref in ((out_ref, inc_ref) if 2 * d < peers else (out_ref,)):
            decay = ref[rows:rows + 1, :]
            for h in range(heads):
                part = pl.ds(h * HP, HP)
                own = ref[part, :]
                got = recv_state[r, part, :].astype(jnp.float32)
                ref[part, :] = jnp.where(reached, decay[:, h:h + 1] * got + own, own)
            ref[rows:] = jnp.where(reached, ref[rows:] * recv_decay[r], ref[rows:])

    send_ref[:rows] = out_ref[:rows].astype(send_ref.dtype)
    send_ref[rows:] = scale_ref[...]
    spread_ref[grp_here] = send_ref[...]
    copies = []
    for offset in range(1, groups):
        copy = pltpu.make_async_remote_copy(
            src_ref=send_ref,
            dst_ref=spread_ref.at[grp_here],
            send_sem=spread_send.at[offset],
            recv_sem=spread_recv.at[grp_here],
            device_id=device(here, lax.rem(grp_here + offset, groups)),
            device_id_type=pl.DeviceIdType.MESH,
        )
        copy.start()
        copies.append(copy)
    for copy in copies:
        copy.wait_send()
    for offset in range(1, groups):
        source = lax.rem(grp_here + groups - offset, groups)
        pltpu.make_async_remote_copy(
            src_ref=send_ref,
            dst_ref=spread_ref.at[source],
            send_sem=spread_send.at[offset],
            recv_sem=spread_recv.at[source],
            device_id=device(here, source),
            device_id_type=pl.DeviceIdType.MESH,
        ).wait_recv()


def _hops(peers):
    d, hops = 1, []
    while d < peers:
        hops.append(d)
        d *= 2
    return hops


def carry_in(total_log, state_t, names, after, scale_packed):
    peers = lax.axis_size("seq")
    groups = lax.axis_size("grp")
    heads, width, lanes = state_t.shape
    rows = heads * width
    decay = jnp.ones((8, lanes), jnp.float32).at[0, :heads].set(jnp.exp(total_log))
    msg = jnp.concatenate([state_t.reshape(rows, lanes), decay], axis=0)
    shape = msg.shape
    hops = len(_hops(peers))
    _, spread = pl.pallas_call(
        functools.partial(scan_kernel, peers, names),
        out_shape=(
            jax.ShapeDtypeStruct(shape, jnp.float32),
            jax.ShapeDtypeStruct((groups, rows + scale_packed.shape[0], lanes), jnp.bfloat16),
        ),
        in_specs=[
            pl.BlockSpec(memory_space=pltpu.VMEM),
            pl.BlockSpec(memory_space=pl.ANY),
            pl.BlockSpec(memory_space=pltpu.VMEM),
        ],
        out_specs=(pl.BlockSpec(memory_space=pltpu.VMEM), pl.BlockSpec(memory_space=pltpu.VMEM)),
        scratch_shapes=[
            pltpu.VMEM(shape, jnp.float32),
            pltpu.VMEM((hops, rows, lanes), jnp.bfloat16),
            pltpu.VMEM((hops, rows, lanes), jnp.bfloat16),
            pltpu.VMEM((hops, 8, lanes), jnp.float32),
            pltpu.VMEM((rows + scale_packed.shape[0], lanes), jnp.bfloat16),
            pltpu.SemaphoreType.DMA((hops,)),
            pltpu.SemaphoreType.DMA((hops,)),
            pltpu.SemaphoreType.DMA((hops,)),
            pltpu.SemaphoreType.DMA((hops,)),
            pltpu.SemaphoreType.DMA((groups,)),
            pltpu.SemaphoreType.DMA((groups,)),
        ],
        compiler_params=pltpu.CompilerParams(collective_id=0, has_side_effects=True),
        cost_estimate=pl.CostEstimate(flops=0, transcendentals=0, bytes_accessed=512 * msg.size * 4),
    )(msg, after, scale_packed)
    return spread


def on_device(
    names,
    mixer_input, step_sizes, decay_rates, skip_gain, input_basis, output_basis, out_weight
):
    heads_here = step_sizes.shape[0]
    tokens_here = step_sizes.shape[1]
    count = tokens_here // GROUP
    channels = mixer_input.reshape(heads_here, HP, count, GROUP)
    log_decay = -(decay_rates[:, None] * step_sizes).reshape(heads_here, count, GROUP)
    steps_blocked = step_sizes.reshape(heads_here, count, GROUP)
    running = jnp.cumsum(log_decay, axis=2)
    basis_in_blocked = input_basis.reshape(count, GROUP, N)
    basis_out_blocked = output_basis.reshape(count, GROUP, N)
    gram = jnp.einsum(
        "cin,cjn->cij", basis_out_blocked, basis_in_blocked, preferred_element_type=jnp.float32
    )
    rows_index = lax.broadcasted_iota(jnp.int32, (GROUP, GROUP), 0)
    cols_index = lax.broadcasted_iota(jnp.int32, (GROUP, GROUP), 1)
    causal = rows_index >= cols_index
    gaps = running[:, :, :, None] - running[:, :, None, :]
    mixing = jnp.where(
        causal,
        gram[None] * jnp.exp(jnp.where(causal, gaps, 0.0)) * steps_blocked[:, :, None, :],
        0.0,
    ).astype(jnp.bfloat16)
    inner = jnp.einsum("hcij,hpcj->hpci", mixing, channels, preferred_element_type=jnp.float32)
    tail_decay = jnp.exp(running[:, :, -1:] - running) * steps_blocked
    weighted_terms = (basis_in_blocked.astype(jnp.float32)[None] * tail_decay[:, :, :, None]).astype(
        jnp.bfloat16
    )
    summaries = jnp.einsum(
        "hcjn,hpcj->chnp", weighted_terms, channels, preferred_element_type=jnp.float32
    )
    block_sums = jnp.sum(log_decay, axis=2)
    block_cum = jnp.cumsum(block_sums, axis=1)
    log_prefix = block_cum - block_sums
    total_log = block_cum[:, -1]
    entering = [jnp.zeros_like(summaries[0])]
    for c in range(1, count + 1):
        reach = log_prefix[:, c] if c < count else total_log
        term = jnp.zeros_like(summaries[0])
        for earlier in range(c):
            weight = jnp.exp(reach - block_cum[:, earlier])
            term = term + weight[:, None, None] * summaries[earlier]
        entering.append(term)
    final_state = entering[count]
    entering = jnp.stack(entering[:count])
    basis_out_wide = basis_out_blocked.astype(jnp.float32)
    within = jnp.exp(running)[:, None]
    direct = skip_gain[:, None, None, None] * channels.astype(jnp.float32)
    from_local = jnp.einsum(
        "cin,chnp->hpci", basis_out_wide, entering, precision=lax.Precision.HIGHEST
    )
    local = (inner + from_local * within + direct).astype(jnp.bfloat16)
    scale = jnp.exp(running + log_prefix[:, :, None]).reshape(heads_here, tokens_here)
    scale_hi = scale.astype(jnp.bfloat16)
    scale_lo = (scale - scale_hi.astype(jnp.float32)).astype(jnp.bfloat16)
    scale_rows = jnp.concatenate([scale_hi, scale_lo], axis=0)
    scale_packed = scale_rows.reshape(-1, 128)
    local_flat = local.reshape(heads_here * HP, tokens_here)
    local_all = lax.all_gather(local_flat, "grp", axis=0, tiled=True)
    spread = carry_in(total_log, jnp.swapaxes(final_state, 1, 2), names, local_flat, scale_packed)
    groups = spread.shape[0]
    carried_t = spread[:, : heads_here * HP].reshape(groups * heads_here * HP, N)
    scale_all = spread[:, heads_here * HP :].reshape(groups, 2 * heads_here, tokens_here)
    result_t = tail(local_all, output_basis, carried_t, scale_all, out_weight.T)
    return result_t.T


def tail_kernel(local_ref, basis_ref, carried_ref, scale_ref, weight_ref, out_ref, acc_ref, mixed_ref):
    g = pl.program_id(0)

    @pl.when(g == 0)
    def _():
        acc_ref[...] = jnp.zeros_like(acc_ref)

    base, tokens = mixed_ref.shape
    per = base // HP
    carry = lax.dot_general(
        carried_ref[...], basis_ref[...], (((1,), (1,)), ((), ())), preferred_element_type=jnp.float32
    )
    scale = scale_ref[pl.ds(0, per), :].astype(jnp.float32) + scale_ref[
        pl.ds(per, per), :
    ].astype(jnp.float32)
    carry = (carry.reshape(per, HP, tokens) * scale[:, None, :]).reshape(base, tokens)
    mixed_ref[...] = (local_ref[pl.ds(0, base), :].astype(jnp.float32) + carry).astype(jnp.bfloat16)
    acc_ref[...] += jnp.dot(weight_ref[...], mixed_ref[...], preferred_element_type=jnp.float32)

    @pl.when(g == pl.num_programs(0) - 1)
    def _():
        out_ref[...] = acc_ref[...].astype(out_ref.dtype)


def tail(local_all, basis, carried_t, scale_all, weight_t):
    channels, tokens = local_all.shape
    features = weight_t.shape[0]
    groups = lax.axis_size("grp")
    per = carried_t.shape[0] // groups // HP
    return pl.pallas_call(
        tail_kernel,
        out_shape=jax.ShapeDtypeStruct((features, tokens), jnp.bfloat16),
        grid=(groups,),
        in_specs=[
            pl.BlockSpec((channels // groups, tokens), lambda g: (g, 0)),
            pl.BlockSpec(basis.shape, lambda g: (0, 0)),
            pl.BlockSpec((per * HP, N), lambda g: (g, 0)),
            pl.BlockSpec((None, 2 * per, tokens), lambda g: (g, 0, 0)),
            pl.BlockSpec((features, per * HP), lambda g: (0, g)),
        ],
        out_specs=pl.BlockSpec((features, tokens), lambda g: (0, 0)),
        scratch_shapes=[
            pltpu.VMEM((features, tokens), jnp.float32),
            pltpu.VMEM((per * HP, tokens), jnp.bfloat16),
        ],
        cost_estimate=pl.CostEstimate(
            flops=2 * tokens * per * HP * groups * (N + features),
            transcendentals=0,
            bytes_accessed=2 * (local_all.size + weight_t.size) + 2 * features * tokens,
        ),
    )(local_all, basis, carried_t, scale_all, weight_t)


def solution(mesh):
    placed = (
        P("grp", "seq"),
        P("grp", "seq"),
        P("grp"),
        P("grp"),
        P("seq", None),
        P("seq", None),
        P(None, "grp"),
    )
    return jax.shard_map(
        functools.partial(on_device, mesh.axis_names), mesh=mesh, in_specs=placed, out_specs=P("seq", "grp"), check_vma=False
    )
```

```python
import functools

import jax
import jax.numpy as jnp
from jax import lax
from jax.experimental import pallas as pl
from jax.experimental.pallas import tpu as pltpu
from jax.sharding import PartitionSpec as P

HP = 64
N = 128
GROUP = 256


def scan_kernel(peers, names, msg_ref, after_ref, scale_ref, out_ref, spread_ref, inc_ref, out_state, recv_state,
                recv_decay, send_ref, send_sem, recv_sem, decay_send, decay_recv, spread_send, spread_recv):
    here = lax.axis_index("seq")
    grp_here = lax.axis_index("grp")
    groups = spread_ref.shape[0]
    rows = msg_ref.shape[0] - 8
    heads = rows // HP

    def device(seq_at, grp_at):
        return tuple(seq_at if name == "seq" else grp_at for name in names)

    offsets = sorted({d % peers for d in _hops(peers)} | {(-d) % peers for d in _hops(peers)})
    barrier = pltpu.get_barrier_semaphore()
    for offset in offsets:
        pl.semaphore_signal(
            barrier, inc=1, device_id=device(lax.rem(here + offset, peers), grp_here),
            device_id_type=pl.DeviceIdType.MESH,
        )
    for offset in range(1, groups):
        pl.semaphore_signal(
            barrier, inc=1, device_id=device(here, lax.rem(grp_here + offset, groups)),
            device_id_type=pl.DeviceIdType.MESH,
        )
    pl.semaphore_wait(barrier, len(offsets) + groups - 1)

    inc_ref[...] = msg_ref[...]
    out_ref[:rows] = jnp.zeros((rows, out_ref.shape[1]), jnp.float32)
    out_ref[rows:] = jnp.ones((8, out_ref.shape[1]), jnp.float32)
    for r, d in enumerate(_hops(peers)):
        target = device(lax.rem(here + d, peers), grp_here)
        out_state[r] = inc_ref[:rows].astype(out_state.dtype)
        state_copy = pltpu.make_async_remote_copy(
            src_ref=out_state.at[r],
            dst_ref=recv_state.at[r],
            send_sem=send_sem.at[r],
            recv_sem=recv_sem.at[r],
            device_id=target,
            device_id_type=pl.DeviceIdType.MESH,
        )
        decay_copy = pltpu.make_async_remote_copy(
            src_ref=inc_ref.at[pl.ds(rows, 8)],
            dst_ref=recv_decay.at[r],
            send_sem=decay_send.at[r],
            recv_sem=decay_recv.at[r],
            device_id=target,
            device_id_type=pl.DeviceIdType.MESH,
        )
        state_copy.start()
        decay_copy.start()
        state_copy.wait()
        decay_copy.wait()
        reached = here >= d
        for ref in ((out_ref, inc_ref) if 2 * d < peers else (out_ref,)):
            decay = ref[rows:rows + 1, :]
            for h in range(heads):
                part = pl.ds(h * HP, HP)
                own = ref[part, :]
                got = recv_state[r, part, :].astype(jnp.float32)
                ref[part, :] = jnp.where(reached, decay[:, h:h + 1] * got + own, own)
            ref[rows:] = jnp.where(reached, ref[rows:] * recv_decay[r], ref[rows:])

    send_ref[:rows] = out_ref[:rows].astype(send_ref.dtype)
    send_ref[rows:] = scale_ref[...]
    spread_ref[grp_here] = send_ref[...]
    copies = []
    for offset in range(1, groups):
        copy = pltpu.make_async_remote_copy(
            src_ref=send_ref,
            dst_ref=spread_ref.at[grp_here],
            send_sem=spread_send.at[offset],
            recv_sem=spread_recv.at[grp_here],
            device_id=device(here, lax.rem(grp_here + offset, groups)),
            device_id_type=pl.DeviceIdType.MESH,
        )
        copy.start()
        copies.append(copy)
    for copy in copies:
        copy.wait_send()
    for offset in range(1, groups):
        source = lax.rem(grp_here + groups - offset, groups)
        pltpu.make_async_remote_copy(
            src_ref=send_ref,
            dst_ref=spread_ref.at[source],
            send_sem=spread_send.at[offset],
            recv_sem=spread_recv.at[source],
            device_id=device(here, source),
            device_id_type=pl.DeviceIdType.MESH,
        ).wait_recv()


def _hops(peers):
    d, hops = 1, []
    while d < peers:
        hops.append(d)
        d *= 2
    return hops


def carry_in(total_log, state_t, names, after, scale_packed):
    peers = lax.axis_size("seq")
    groups = lax.axis_size("grp")
    heads, width, lanes = state_t.shape
    rows = heads * width
    decay = jnp.ones((8, lanes), jnp.float32).at[0, :heads].set(jnp.exp(total_log))
    msg = jnp.concatenate([state_t.reshape(rows, lanes), decay], axis=0)
    shape = msg.shape
    hops = len(_hops(peers))
    _, spread = pl.pallas_call(
        functools.partial(scan_kernel, peers, names),
        out_shape=(
            jax.ShapeDtypeStruct(shape, jnp.float32),
            jax.ShapeDtypeStruct((groups, rows + scale_packed.shape[0], lanes), jnp.bfloat16),
        ),
        in_specs=[
            pl.BlockSpec(memory_space=pltpu.VMEM),
            pl.BlockSpec(memory_space=pl.ANY),
            pl.BlockSpec(memory_space=pltpu.VMEM),
        ],
        out_specs=(pl.BlockSpec(memory_space=pltpu.VMEM), pl.BlockSpec(memory_space=pltpu.VMEM)),
        scratch_shapes=[
            pltpu.VMEM(shape, jnp.float32),
            pltpu.VMEM((hops, rows, lanes), jnp.bfloat16),
            pltpu.VMEM((hops, rows, lanes), jnp.bfloat16),
            pltpu.VMEM((hops, 8, lanes), jnp.float32),
            pltpu.VMEM((rows + scale_packed.shape[0], lanes), jnp.bfloat16),
            pltpu.SemaphoreType.DMA((hops,)),
            pltpu.SemaphoreType.DMA((hops,)),
            pltpu.SemaphoreType.DMA((hops,)),
            pltpu.SemaphoreType.DMA((hops,)),
            pltpu.SemaphoreType.DMA((groups,)),
            pltpu.SemaphoreType.DMA((groups,)),
        ],
        compiler_params=pltpu.CompilerParams(collective_id=0, has_side_effects=True),
        cost_estimate=pl.CostEstimate(flops=0, transcendentals=0, bytes_accessed=512 * msg.size * 4),
    )(msg, after, scale_packed)
    return spread


def on_device(
    names,
    mixer_input, step_sizes, decay_rates, skip_gain, input_basis, output_basis, out_weight
):
    heads_here = step_sizes.shape[0]
    tokens_here = step_sizes.shape[1]
    count = tokens_here // GROUP
    channels = mixer_input.reshape(heads_here, HP, count, GROUP)
    log_decay = -(decay_rates[:, None] * step_sizes).reshape(heads_here, count, GROUP)
    steps_blocked = step_sizes.reshape(heads_here, count, GROUP)
    running = jnp.cumsum(log_decay, axis=2)
    basis_in_blocked = input_basis.reshape(count, GROUP, N)
    basis_out_blocked = output_basis.reshape(count, GROUP, N)
    gram = jnp.einsum(
        "cin,cjn->cij", basis_out_blocked, basis_in_blocked, preferred_element_type=jnp.float32
    )
    rows_index = lax.broadcasted_iota(jnp.int32, (GROUP, GROUP), 0)
    cols_index = lax.broadcasted_iota(jnp.int32, (GROUP, GROUP), 1)
    causal = rows_index >= cols_index
    gaps = running[:, :, :, None] - running[:, :, None, :]
    mixing = jnp.where(
        causal,
        gram[None] * jnp.exp(jnp.where(causal, gaps, 0.0)) * steps_blocked[:, :, None, :],
        0.0,
    ).astype(jnp.bfloat16)
    inner = jnp.einsum("hcij,hpcj->hpci", mixing, channels, preferred_element_type=jnp.float32)
    tail_decay = jnp.exp(running[:, :, -1:] - running) * steps_blocked
    weighted_terms = (basis_in_blocked.astype(jnp.float32)[None] * tail_decay[:, :, :, None]).astype(
        jnp.bfloat16
    )
    summaries = jnp.einsum(
        "hcjn,hpcj->chnp", weighted_terms, channels, preferred_element_type=jnp.float32
    )
    block_sums = jnp.sum(log_decay, axis=2)
    block_cum = jnp.cumsum(block_sums, axis=1)
    log_prefix = block_cum - block_sums
    total_log = block_cum[:, -1]
    entering = [jnp.zeros_like(summaries[0])]
    for c in range(1, count + 1):
        reach = log_prefix[:, c] if c < count else total_log
        term = jnp.zeros_like(summaries[0])
        for earlier in range(c):
            weight = jnp.exp(reach - block_cum[:, earlier])
            term = term + weight[:, None, None] * summaries[earlier]
        entering.append(term)
    final_state = entering[count]
    entering = jnp.stack(entering[:count])
    basis_out_wide = basis_out_blocked.astype(jnp.float32)
    within = jnp.exp(running)[:, None]
    direct = skip_gain[:, None, None, None] * channels.astype(jnp.float32)
    from_local = jnp.einsum(
        "cin,chnp->hpci", basis_out_wide, entering, precision=lax.Precision.HIGHEST
    )
    local = (inner + from_local * within + direct).astype(jnp.bfloat16)
    scale = jnp.exp(running + log_prefix[:, :, None]).reshape(heads_here, tokens_here)
    scale_hi = scale.astype(jnp.bfloat16)
    scale_lo = (scale - scale_hi.astype(jnp.float32)).astype(jnp.bfloat16)
    scale_rows = jnp.concatenate([scale_hi, scale_lo], axis=0)
    scale_packed = scale_rows.reshape(-1, 128)
    local_flat = local.reshape(heads_here * HP, tokens_here)
    local_all = lax.all_gather(local_flat, "grp", axis=0, tiled=True)
    spread = carry_in(total_log, jnp.swapaxes(final_state, 1, 2), names, local_flat, scale_packed)
    result_t = tail(local_all, output_basis, spread, out_weight.T)
    return result_t.T


def tail_kernel(local_ref, basis_ref, carried_ref, scale_ref, weight_ref, out_ref, acc_ref, mixed_ref):
    g = pl.program_id(0)

    @pl.when(g == 0)
    def _():
        acc_ref[...] = jnp.zeros_like(acc_ref)

    base, tokens = mixed_ref.shape
    per = base // HP
    tiles = tokens // 128
    carry = lax.dot_general(
        carried_ref[...], basis_ref[...], (((1,), (1,)), ((), ())), preferred_element_type=jnp.float32
    )
    for h in range(per):
        for k in range(tiles):
            rows, lanes = slice(h * HP, (h + 1) * HP), slice(k * 128, (k + 1) * 128)
            scale = scale_ref[pl.ds(h * tiles + k, 1), :].astype(jnp.float32) + scale_ref[
                pl.ds((per + h) * tiles + k, 1), :
            ].astype(jnp.float32)
            mixed_ref[rows, lanes] = (
                local_ref[rows, lanes].astype(jnp.float32) + carry[rows, lanes] * scale
            ).astype(jnp.bfloat16)
    acc_ref[...] += jnp.dot(weight_ref[...], mixed_ref[...], preferred_element_type=jnp.float32)

    @pl.when(g == pl.num_programs(0) - 1)
    def _():
        out_ref[...] = acc_ref[...].astype(out_ref.dtype)


def tail(local_all, basis, spread, weight_t):
    channels, tokens = local_all.shape
    features = weight_t.shape[0]
    groups = lax.axis_size("grp")
    per = channels // groups // HP
    packed = 2 * per * tokens // 128
    return pl.pallas_call(
        tail_kernel,
        out_shape=jax.ShapeDtypeStruct((features, tokens), jnp.bfloat16),
        grid=(groups,),
        in_specs=[
            pl.BlockSpec((channels // groups, tokens), lambda g: (g, 0)),
            pl.BlockSpec(basis.shape, lambda g: (0, 0)),
            pl.BlockSpec((None, per * HP, N), lambda g: (g, 0, 0)),
            pl.BlockSpec((None, packed, N), lambda g: (g, per * HP // packed, 0)),
            pl.BlockSpec((features, per * HP), lambda g: (0, g)),
        ],
        out_specs=pl.BlockSpec((features, tokens), lambda g: (0, 0)),
        scratch_shapes=[
            pltpu.VMEM((features, tokens), jnp.float32),
            pltpu.VMEM((per * HP, tokens), jnp.bfloat16),
        ],
        cost_estimate=pl.CostEstimate(
            flops=2 * tokens * per * HP * groups * (N + features),
            transcendentals=0,
            bytes_accessed=2 * (local_all.size + weight_t.size) + 2 * features * tokens,
        ),
    )(local_all, basis, spread, spread, weight_t)


def solution(mesh):
    placed = (
        P("grp", "seq"),
        P("grp", "seq"),
        P("grp"),
        P("grp"),
        P("seq", None),
        P("seq", None),
        P(None, "grp"),
    )
    return jax.shard_map(
        functools.partial(on_device, mesh.axis_names), mesh=mesh, in_specs=placed, out_specs=P("seq", "grp"), check_vma=False
    )
```

```python
import functools

import jax
import jax.numpy as jnp
from jax import lax
from jax.experimental import pallas as pl
from jax.experimental.pallas import tpu as pltpu
from jax.sharding import PartitionSpec as P

HP = 64
N = 128
GROUP = 256


def scan_kernel(peers, names, msg_ref, after_ref, out_ref, spread_ref, inc_ref, out_state, recv_state,
                recv_decay, send_ref, send_sem, recv_sem, decay_send, decay_recv, spread_send, spread_recv):
    here = lax.axis_index("seq")
    grp_here = lax.axis_index("grp")
    groups = spread_ref.shape[0]
    rows = msg_ref.shape[0] - 8
    heads = rows // HP

    def device(seq_at, grp_at):
        return tuple(seq_at if name == "seq" else grp_at for name in names)

    offsets = sorted({d % peers for d in _hops(peers)} | {(-d) % peers for d in _hops(peers)})
    barrier = pltpu.get_barrier_semaphore()
    for offset in offsets:
        pl.semaphore_signal(
            barrier, inc=1, device_id=device(lax.rem(here + offset, peers), grp_here),
            device_id_type=pl.DeviceIdType.MESH,
        )
    for offset in range(1, groups):
        pl.semaphore_signal(
            barrier, inc=1, device_id=device(here, lax.rem(grp_here + offset, groups)),
            device_id_type=pl.DeviceIdType.MESH,
        )
    pl.semaphore_wait(barrier, len(offsets) + groups - 1)

    inc_ref[...] = msg_ref[...]
    out_ref[:rows] = jnp.zeros((rows, out_ref.shape[1]), jnp.float32)
    out_ref[rows:] = jnp.ones((8, out_ref.shape[1]), jnp.float32)
    for r, d in enumerate(_hops(peers)):
        target = device(lax.rem(here + d, peers), grp_here)
        out_state[r] = inc_ref[:rows].astype(out_state.dtype)
        state_copy = pltpu.make_async_remote_copy(
            src_ref=out_state.at[r],
            dst_ref=recv_state.at[r],
            send_sem=send_sem.at[r],
            recv_sem=recv_sem.at[r],
            device_id=target,
            device_id_type=pl.DeviceIdType.MESH,
        )
        decay_copy = pltpu.make_async_remote_copy(
            src_ref=inc_ref.at[pl.ds(rows, 8)],
            dst_ref=recv_decay.at[r],
            send_sem=decay_send.at[r],
            recv_sem=decay_recv.at[r],
            device_id=target,
            device_id_type=pl.DeviceIdType.MESH,
        )
        state_copy.start()
        decay_copy.start()
        state_copy.wait()
        decay_copy.wait()
        reached = here >= d
        for ref in ((out_ref, inc_ref) if 2 * d < peers else (out_ref,)):
            decay = ref[rows:rows + 1, :]
            for h in range(heads):
                part = pl.ds(h * HP, HP)
                own = ref[part, :]
                got = recv_state[r, part, :].astype(jnp.float32)
                ref[part, :] = jnp.where(reached, decay[:, h:h + 1] * got + own, own)
            ref[rows:] = jnp.where(reached, ref[rows:] * recv_decay[r], ref[rows:])

    send_ref[...] = out_ref[:rows].astype(send_ref.dtype)
    spread_ref[grp_here] = out_ref[:rows].astype(spread_ref.dtype)
    partner = grp_here + 1 - 2 * lax.rem(grp_here, 2)

    def spread_copy(slot, target, sem):
        return pltpu.make_async_remote_copy(
            src_ref=send_ref if slot is None else spread_ref.at[slot],
            dst_ref=spread_ref.at[grp_here if slot is None else slot],
            send_sem=sem,
            recv_sem=spread_recv.at[grp_here if slot is None else slot],
            device_id=device(here, target),
            device_id_type=pl.DeviceIdType.MESH,
        )

    def arriving(slot, source):
        return pltpu.make_async_remote_copy(
            src_ref=send_ref,
            dst_ref=spread_ref.at[slot],
            send_sem=spread_send.at[0],
            recv_sem=spread_recv.at[slot],
            device_id=device(here, source),
            device_id_type=pl.DeviceIdType.MESH,
        )

    chips = groups // 2
    copies = [spread_copy(None, partner, spread_send.at[0])]
    for k in range(1, chips):
        copies.append(spread_copy(None, lax.rem(grp_here + 2 * k, groups), spread_send.at[k]))
    for copy in copies:
        copy.start()
    arriving(partner, partner).wait_recv()
    forwards = []
    for k in range(1, chips):
        source = lax.rem(grp_here + groups - 2 * k, groups)
        arriving(source, source).wait_recv()
        forward = spread_copy(source, partner, spread_send.at[chips - 1 + k])
        forward.start()
        forwards.append(forward)
    for k in range(1, chips):
        slot = lax.rem(partner + groups - 2 * k, groups)
        arriving(slot, partner).wait_recv()
    for copy in copies + forwards:
        copy.wait_send()


def _hops(peers):
    d, hops = 1, []
    while d < peers:
        hops.append(d)
        d *= 2
    return hops


def carry_in(total_log, state_t, names, after):
    peers = lax.axis_size("seq")
    groups = lax.axis_size("grp")
    heads, width, lanes = state_t.shape
    rows = heads * width
    decay = jnp.ones((8, lanes), jnp.float32).at[0, :heads].set(jnp.exp(total_log))
    msg = jnp.concatenate([state_t.reshape(rows, lanes), decay], axis=0)
    shape = msg.shape
    hops = len(_hops(peers))
    _, spread = pl.pallas_call(
        functools.partial(scan_kernel, peers, names),
        out_shape=(
            jax.ShapeDtypeStruct(shape, jnp.float32),
            jax.ShapeDtypeStruct((groups, rows, lanes), jnp.bfloat16),
        ),
        in_specs=[pl.BlockSpec(memory_space=pltpu.VMEM), pl.BlockSpec(memory_space=pl.ANY)],
        out_specs=(pl.BlockSpec(memory_space=pltpu.VMEM), pl.BlockSpec(memory_space=pltpu.VMEM)),
        scratch_shapes=[
            pltpu.VMEM(shape, jnp.float32),
            pltpu.VMEM((hops, rows, lanes), jnp.bfloat16),
            pltpu.VMEM((hops, rows, lanes), jnp.bfloat16),
            pltpu.VMEM((hops, 8, lanes), jnp.float32),
            pltpu.VMEM((rows, lanes), jnp.bfloat16),
            pltpu.SemaphoreType.DMA((hops,)),
            pltpu.SemaphoreType.DMA((hops,)),
            pltpu.SemaphoreType.DMA((hops,)),
            pltpu.SemaphoreType.DMA((hops,)),
            pltpu.SemaphoreType.DMA((groups,)),
            pltpu.SemaphoreType.DMA((groups,)),
        ],
        compiler_params=pltpu.CompilerParams(collective_id=0, has_side_effects=True),
        cost_estimate=pl.CostEstimate(flops=0, transcendentals=0, bytes_accessed=512 * msg.size * 4),
    )(msg, after)
    return spread.reshape(groups * rows, lanes)


def on_device(
    names,
    mixer_input, step_sizes, decay_rates, skip_gain, input_basis, output_basis, out_weight
):
    heads_here = step_sizes.shape[0]
    tokens_here = step_sizes.shape[1]
    count = tokens_here // GROUP
    channels = mixer_input.reshape(heads_here, HP, count, GROUP)
    log_decay = -(decay_rates[:, None] * step_sizes).reshape(heads_here, count, GROUP)
    steps_blocked = step_sizes.reshape(heads_here, count, GROUP)
    running = jnp.cumsum(log_decay, axis=2)
    basis_in_blocked = input_basis.reshape(count, GROUP, N)
    basis_out_blocked = output_basis.reshape(count, GROUP, N)
    gram = jnp.einsum(
        "cin,cjn->cij", basis_out_blocked, basis_in_blocked, preferred_element_type=jnp.float32
    )
    rows_index = lax.broadcasted_iota(jnp.int32, (GROUP, GROUP), 0)
    cols_index = lax.broadcasted_iota(jnp.int32, (GROUP, GROUP), 1)
    causal = rows_index >= cols_index
    gaps = running[:, :, :, None] - running[:, :, None, :]
    mixing = jnp.where(
        causal,
        gram[None] * jnp.exp(jnp.where(causal, gaps, 0.0)) * steps_blocked[:, :, None, :],
        0.0,
    ).astype(jnp.bfloat16)
    inner = jnp.einsum("hcij,hpcj->hpci", mixing, channels, preferred_element_type=jnp.float32)
    tail_decay = jnp.exp(running[:, :, -1:] - running) * steps_blocked
    weighted_terms = (basis_in_blocked.astype(jnp.float32)[None] * tail_decay[:, :, :, None]).astype(
        jnp.bfloat16
    )
    summaries = jnp.einsum(
        "hcjn,hpcj->chnp", weighted_terms, channels, preferred_element_type=jnp.float32
    )
    block_sums = jnp.sum(log_decay, axis=2)
    block_cum = jnp.cumsum(block_sums, axis=1)
    log_prefix = block_cum - block_sums
    total_log = block_cum[:, -1]
    entering = [jnp.zeros_like(summaries[0])]
    for c in range(1, count + 1):
        reach = log_prefix[:, c] if c < count else total_log
        term = jnp.zeros_like(summaries[0])
        for earlier in range(c):
            weight = jnp.exp(reach - block_cum[:, earlier])
            term = term + weight[:, None, None] * summaries[earlier]
        entering.append(term)
    final_state = entering[count]
    entering = jnp.stack(entering[:count])
    basis_out_wide = basis_out_blocked.astype(jnp.float32)
    within = jnp.exp(running)[:, None]
    direct = skip_gain[:, None, None, None] * channels.astype(jnp.float32)
    from_local = jnp.einsum(
        "cin,chnp->hpci", basis_out_wide, entering, precision=lax.Precision.HIGHEST
    )
    local = (inner + from_local * within + direct).astype(jnp.bfloat16)
    scale = jnp.exp(running + log_prefix[:, :, None]).reshape(heads_here, tokens_here)
    scale_hi = scale.astype(jnp.bfloat16)
    scale_lo = (scale - scale_hi.astype(jnp.float32)).astype(jnp.bfloat16)
    extra = 32 - 2 * heads_here
    local_ext = jnp.concatenate(
        [
            local.reshape(heads_here * HP, tokens_here),
            scale_hi,
            scale_lo,
            jnp.zeros((extra, tokens_here), jnp.bfloat16),
        ],
        axis=0,
    )
    local_all = lax.all_gather(local_ext, "grp", axis=0, tiled=True)
    carried_t = carry_in(total_log, jnp.swapaxes(final_state, 1, 2), names, local_ext)
    result_t = tail(local_all, output_basis, carried_t, out_weight.T)
    return result_t.T


def tail_kernel(local_ref, basis_ref, carried_ref, weight_ref, out_ref, acc_ref, mixed_ref):
    g = pl.program_id(0)

    @pl.when(g == 0)
    def _():
        acc_ref[...] = jnp.zeros_like(acc_ref)

    base, tokens = mixed_ref.shape
    per = base // HP
    carry = lax.dot_general(
        carried_ref[...], basis_ref[...], (((1,), (1,)), ((), ())), preferred_element_type=jnp.float32
    )
    scale = local_ref[pl.ds(base, per), :].astype(jnp.float32) + local_ref[
        pl.ds(base + per, per), :
    ].astype(jnp.float32)
    carry = (carry.reshape(per, HP, tokens) * scale[:, None, :]).reshape(base, tokens)
    mixed_ref[...] = (local_ref[pl.ds(0, base), :].astype(jnp.float32) + carry).astype(jnp.bfloat16)
    acc_ref[...] += jnp.dot(weight_ref[...], mixed_ref[...], preferred_element_type=jnp.float32)

    @pl.when(g == pl.num_programs(0) - 1)
    def _():
        out_ref[...] = acc_ref[...].astype(out_ref.dtype)


def tail(local_all, basis, carried_t, weight_t):
    channels, tokens = local_all.shape
    features = weight_t.shape[0]
    groups = lax.axis_size("grp")
    per = carried_t.shape[0] // groups // HP
    return pl.pallas_call(
        tail_kernel,
        out_shape=jax.ShapeDtypeStruct((features, tokens), jnp.bfloat16),
        grid=(groups,),
        in_specs=[
            pl.BlockSpec((channels // groups, tokens), lambda g: (g, 0)),
            pl.BlockSpec(basis.shape, lambda g: (0, 0)),
            pl.BlockSpec((per * HP, N), lambda g: (g, 0)),
            pl.BlockSpec((features, per * HP), lambda g: (0, g)),
        ],
        out_specs=pl.BlockSpec((features, tokens), lambda g: (0, 0)),
        scratch_shapes=[
            pltpu.VMEM((features, tokens), jnp.float32),
            pltpu.VMEM((per * HP, tokens), jnp.bfloat16),
        ],
        cost_estimate=pl.CostEstimate(
            flops=2 * tokens * per * HP * groups * (N + features),
            transcendentals=0,
            bytes_accessed=2 * (local_all.size + weight_t.size) + 2 * features * tokens,
        ),
    )(local_all, basis, carried_t, weight_t)


def solution(mesh):
    placed = (
        P("grp", "seq"),
        P("grp", "seq"),
        P("grp"),
        P("grp"),
        P("seq", None),
        P("seq", None),
        P(None, "grp"),
    )
    return jax.shard_map(
        functools.partial(on_device, mesh.axis_names), mesh=mesh, in_specs=placed, out_specs=P("seq", "grp"), check_vma=False
    )
```

```python
import functools

import jax
import jax.numpy as jnp
from jax import lax
from jax.experimental import pallas as pl
from jax.experimental.pallas import tpu as pltpu
from jax.sharding import PartitionSpec as P

HP = 64
N = 128
GROUP = 256


def scan_kernel(peers, names, msg_ref, after_ref, scale_ref, out_ref, spread_ref, inc_ref, out_state, recv_state,
                recv_decay, send_ref, send_sem, recv_sem, decay_send, decay_recv, spread_send, spread_recv):
    here = lax.axis_index("seq")
    grp_here = lax.axis_index("grp")
    groups = spread_ref.shape[0]
    rows = msg_ref.shape[0] - 8
    heads = rows // HP

    def device(seq_at, grp_at):
        return tuple(seq_at if name == "seq" else grp_at for name in names)

    offsets = sorted({d % peers for d in _hops(peers)} | {(-d) % peers for d in _hops(peers)})
    barrier = pltpu.get_barrier_semaphore()
    for offset in offsets:
        pl.semaphore_signal(
            barrier, inc=1, device_id=device(lax.rem(here + offset, peers), grp_here),
            device_id_type=pl.DeviceIdType.MESH,
        )
    for offset in range(1, groups):
        pl.semaphore_signal(
            barrier, inc=1, device_id=device(here, lax.rem(grp_here + offset, groups)),
            device_id_type=pl.DeviceIdType.MESH,
        )
    pl.semaphore_wait(barrier, len(offsets) + groups - 1)

    inc_ref[...] = msg_ref[...]
    out_ref[:rows] = jnp.zeros((rows, out_ref.shape[1]), jnp.float32)
    out_ref[rows:] = jnp.ones((8, out_ref.shape[1]), jnp.float32)
    for r, d in enumerate(_hops(peers)):
        target = device(lax.rem(here + d, peers), grp_here)
        out_state[r] = inc_ref[:rows].astype(out_state.dtype)
        state_copy = pltpu.make_async_remote_copy(
            src_ref=out_state.at[r],
            dst_ref=recv_state.at[r],
            send_sem=send_sem.at[r],
            recv_sem=recv_sem.at[r],
            device_id=target,
            device_id_type=pl.DeviceIdType.MESH,
        )
        decay_copy = pltpu.make_async_remote_copy(
            src_ref=inc_ref.at[pl.ds(rows, 8)],
            dst_ref=recv_decay.at[r],
            send_sem=decay_send.at[r],
            recv_sem=decay_recv.at[r],
            device_id=target,
            device_id_type=pl.DeviceIdType.MESH,
        )
        state_copy.start()
        decay_copy.start()
        state_copy.wait()
        decay_copy.wait()
        reached = here >= d
        for ref in ((out_ref, inc_ref) if 2 * d < peers else (out_ref,)):
            decay = ref[rows:rows + 1, :]
            for h in range(heads):
                part = pl.ds(h * HP, HP)
                own = ref[part, :]
                got = recv_state[r, part, :].astype(jnp.float32)
                ref[part, :] = jnp.where(reached, decay[:, h:h + 1] * got + own, own)
            ref[rows:] = jnp.where(reached, ref[rows:] * recv_decay[r], ref[rows:])

    send_ref[:rows] = out_ref[:rows].astype(send_ref.dtype)
    send_ref[rows:] = scale_ref[...]
    spread_ref[grp_here] = send_ref[...]
    partner = grp_here + 1 - 2 * lax.rem(grp_here, 2)

    def spread_copy(slot, target, sem):
        return pltpu.make_async_remote_copy(
            src_ref=send_ref if slot is None else spread_ref.at[slot],
            dst_ref=spread_ref.at[grp_here if slot is None else slot],
            send_sem=sem,
            recv_sem=spread_recv.at[grp_here if slot is None else slot],
            device_id=device(here, target),
            device_id_type=pl.DeviceIdType.MESH,
        )

    def arriving(slot, source):
        return pltpu.make_async_remote_copy(
            src_ref=send_ref,
            dst_ref=spread_ref.at[slot],
            send_sem=spread_send.at[0],
            recv_sem=spread_recv.at[slot],
            device_id=device(here, source),
            device_id_type=pl.DeviceIdType.MESH,
        )

    chips = groups // 2
    copies = [spread_copy(None, partner, spread_send.at[0])]
    for k in range(1, chips):
        copies.append(spread_copy(None, lax.rem(grp_here + 2 * k, groups), spread_send.at[k]))
    for copy in copies:
        copy.start()
    arriving(partner, partner).wait_recv()
    forwards = []
    for k in range(1, chips):
        source = lax.rem(grp_here + groups - 2 * k, groups)
        arriving(source, source).wait_recv()
        forward = spread_copy(source, partner, spread_send.at[chips - 1 + k])
        forward.start()
        forwards.append(forward)
    for k in range(1, chips):
        slot = lax.rem(partner + groups - 2 * k, groups)
        arriving(slot, partner).wait_recv()
    for copy in copies + forwards:
        copy.wait_send()


def _hops(peers):
    d, hops = 1, []
    while d < peers:
        hops.append(d)
        d *= 2
    return hops


def carry_in(total_log, state_t, names, after, scale_packed):
    peers = lax.axis_size("seq")
    groups = lax.axis_size("grp")
    heads, width, lanes = state_t.shape
    rows = heads * width
    decay = jnp.ones((8, lanes), jnp.float32).at[0, :heads].set(jnp.exp(total_log))
    msg = jnp.concatenate([state_t.reshape(rows, lanes), decay], axis=0)
    shape = msg.shape
    hops = len(_hops(peers))
    _, spread = pl.pallas_call(
        functools.partial(scan_kernel, peers, names),
        out_shape=(
            jax.ShapeDtypeStruct(shape, jnp.float32),
            jax.ShapeDtypeStruct((groups, rows + scale_packed.shape[0], lanes), jnp.bfloat16),
        ),
        in_specs=[
            pl.BlockSpec(memory_space=pltpu.VMEM),
            pl.BlockSpec(memory_space=pl.ANY),
            pl.BlockSpec(memory_space=pltpu.VMEM),
        ],
        out_specs=(pl.BlockSpec(memory_space=pltpu.VMEM), pl.BlockSpec(memory_space=pltpu.VMEM)),
        scratch_shapes=[
            pltpu.VMEM(shape, jnp.float32),
            pltpu.VMEM((hops, rows, lanes), jnp.bfloat16),
            pltpu.VMEM((hops, rows, lanes), jnp.bfloat16),
            pltpu.VMEM((hops, 8, lanes), jnp.float32),
            pltpu.VMEM((rows + scale_packed.shape[0], lanes), jnp.bfloat16),
            pltpu.SemaphoreType.DMA((hops,)),
            pltpu.SemaphoreType.DMA((hops,)),
            pltpu.SemaphoreType.DMA((hops,)),
            pltpu.SemaphoreType.DMA((hops,)),
            pltpu.SemaphoreType.DMA((groups,)),
            pltpu.SemaphoreType.DMA((groups,)),
        ],
        compiler_params=pltpu.CompilerParams(collective_id=0, has_side_effects=True),
        cost_estimate=pl.CostEstimate(flops=0, transcendentals=0, bytes_accessed=512 * msg.size * 4),
    )(msg, after, scale_packed)
    return spread


def on_device(
    names,
    mixer_input, step_sizes, decay_rates, skip_gain, input_basis, output_basis, out_weight
):
    heads_here = step_sizes.shape[0]
    tokens_here = step_sizes.shape[1]
    count = tokens_here // GROUP
    channels = mixer_input.reshape(heads_here, HP, count, GROUP)
    log_decay = -(decay_rates[:, None] * step_sizes).reshape(heads_here, count, GROUP)
    steps_blocked = step_sizes.reshape(heads_here, count, GROUP)
    running = jnp.cumsum(log_decay, axis=2)
    basis_in_blocked = input_basis.reshape(count, GROUP, N)
    basis_out_blocked = output_basis.reshape(count, GROUP, N)
    gram = jnp.einsum(
        "cin,cjn->cij", basis_out_blocked, basis_in_blocked, preferred_element_type=jnp.float32
    )
    rows_index = lax.broadcasted_iota(jnp.int32, (GROUP, GROUP), 0)
    cols_index = lax.broadcasted_iota(jnp.int32, (GROUP, GROUP), 1)
    causal = rows_index >= cols_index
    gaps = running[:, :, :, None] - running[:, :, None, :]
    mixing = jnp.where(
        causal,
        gram[None] * jnp.exp(jnp.where(causal, gaps, 0.0)) * steps_blocked[:, :, None, :],
        0.0,
    ).astype(jnp.bfloat16)
    inner = jnp.einsum("hcij,hpcj->hpci", mixing, channels, preferred_element_type=jnp.float32)
    tail_decay = jnp.exp(running[:, :, -1:] - running) * steps_blocked
    weighted_terms = (basis_in_blocked.astype(jnp.float32)[None] * tail_decay[:, :, :, None]).astype(
        jnp.bfloat16
    )
    summaries = jnp.einsum(
        "hcjn,hpcj->chnp", weighted_terms, channels, preferred_element_type=jnp.float32
    )
    block_sums = jnp.sum(log_decay, axis=2)
    block_cum = jnp.cumsum(block_sums, axis=1)
    log_prefix = block_cum - block_sums
    total_log = block_cum[:, -1]
    entering = [jnp.zeros_like(summaries[0])]
    for c in range(1, count + 1):
        reach = log_prefix[:, c] if c < count else total_log
        term = jnp.zeros_like(summaries[0])
        for earlier in range(c):
            weight = jnp.exp(reach - block_cum[:, earlier])
            term = term + weight[:, None, None] * summaries[earlier]
        entering.append(term)
    final_state = entering[count]
    entering = jnp.stack(entering[:count])
    basis_out_wide = basis_out_blocked.astype(jnp.float32)
    within = jnp.exp(running)[:, None]
    direct = skip_gain[:, None, None, None] * channels.astype(jnp.float32)
    from_local = jnp.einsum(
        "cin,chnp->hpci", basis_out_wide, entering, precision=lax.Precision.HIGHEST
    )
    local = (inner + from_local * within + direct).astype(jnp.bfloat16)
    scale = jnp.exp(running + log_prefix[:, :, None]).reshape(heads_here, tokens_here)
    scale_hi = scale.astype(jnp.bfloat16)
    scale_lo = (scale - scale_hi.astype(jnp.float32)).astype(jnp.bfloat16)
    scale_rows = jnp.concatenate([scale_hi, scale_lo], axis=0)
    scale_packed = scale_rows.reshape(-1, 128)
    local_flat = local.reshape(heads_here * HP, tokens_here)
    local_all = lax.all_gather(local_flat, "grp", axis=0, tiled=True)
    spread = carry_in(total_log, jnp.swapaxes(final_state, 1, 2), names, local_flat, scale_packed)
    result_t = tail(local_all, output_basis, spread, out_weight.T)
    return result_t.T


def tail_kernel(local_ref, basis_ref, carried_ref, scale_ref, weight_ref, out_ref, acc_ref, mixed_ref):
    g = pl.program_id(0)

    @pl.when(g == 0)
    def _():
        acc_ref[...] = jnp.zeros_like(acc_ref)

    base, tokens = mixed_ref.shape
    per = base // HP
    tiles = tokens // 128
    carry = lax.dot_general(
        carried_ref[...], basis_ref[...], (((1,), (1,)), ((), ())), preferred_element_type=jnp.float32
    )
    for h in range(per):
        for k in range(tiles):
            rows, lanes = slice(h * HP, (h + 1) * HP), slice(k * 128, (k + 1) * 128)
            scale = scale_ref[pl.ds(h * tiles + k, 1), :].astype(jnp.float32) + scale_ref[
                pl.ds((per + h) * tiles + k, 1), :
            ].astype(jnp.float32)
            mixed_ref[rows, lanes] = (
                local_ref[rows, lanes].astype(jnp.float32) + carry[rows, lanes] * scale
            ).astype(jnp.bfloat16)
    acc_ref[...] += jnp.dot(weight_ref[...], mixed_ref[...], preferred_element_type=jnp.float32)

    @pl.when(g == pl.num_programs(0) - 1)
    def _():
        out_ref[...] = acc_ref[...].astype(out_ref.dtype)


def tail(local_all, basis, spread, weight_t):
    channels, tokens = local_all.shape
    features = weight_t.shape[0]
    groups = lax.axis_size("grp")
    per = channels // groups // HP
    packed = 2 * per * tokens // 128
    return pl.pallas_call(
        tail_kernel,
        out_shape=jax.ShapeDtypeStruct((features, tokens), jnp.bfloat16),
        grid=(groups,),
        in_specs=[
            pl.BlockSpec((channels // groups, tokens), lambda g: (g, 0)),
            pl.BlockSpec(basis.shape, lambda g: (0, 0)),
            pl.BlockSpec((None, per * HP, N), lambda g: (g, 0, 0)),
            pl.BlockSpec((None, packed, N), lambda g: (g, per * HP // packed, 0)),
            pl.BlockSpec((features, per * HP), lambda g: (0, g)),
        ],
        out_specs=pl.BlockSpec((features, tokens), lambda g: (0, 0)),
        scratch_shapes=[
            pltpu.VMEM((features, tokens), jnp.float32),
            pltpu.VMEM((per * HP, tokens), jnp.bfloat16),
        ],
        cost_estimate=pl.CostEstimate(
            flops=2 * tokens * per * HP * groups * (N + features),
            transcendentals=0,
            bytes_accessed=2 * (local_all.size + weight_t.size) + 2 * features * tokens,
        ),
    )(local_all, basis, spread, spread, weight_t)


def solution(mesh):
    placed = (
        P("grp", "seq"),
        P("grp", "seq"),
        P("grp"),
        P("grp"),
        P("seq", None),
        P("seq", None),
        P(None, "grp"),
    )
    return jax.shard_map(
        functools.partial(on_device, mesh.axis_names), mesh=mesh, in_specs=placed, out_specs=P("seq", "grp"), check_vma=False
    )
```

```python
import functools

import jax
import jax.numpy as jnp
from jax import lax
from jax.experimental import pallas as pl
from jax.experimental.pallas import tpu as pltpu
from jax.sharding import PartitionSpec as P

HP = 64
N = 128
GROUP = 256


def scan_kernel(peers, names, msg_ref, after_ref, scale_ref, out_ref, spread_ref, inc_ref, out_state, recv_state,
                recv_decay, send_ref, send_sem, recv_sem, decay_send, decay_recv, spread_send, spread_recv):
    here = lax.axis_index("seq")
    grp_here = lax.axis_index("grp")
    groups = spread_ref.shape[0]
    rows = msg_ref.shape[0] - 8
    heads = rows // HP

    def device(seq_at, grp_at):
        return tuple(seq_at if name == "seq" else grp_at for name in names)

    offsets = sorted({d % peers for d in _hops(peers)} | {(-d) % peers for d in _hops(peers)})
    barrier = pltpu.get_barrier_semaphore()
    for offset in offsets:
        pl.semaphore_signal(
            barrier, inc=1, device_id=device(lax.rem(here + offset, peers), grp_here),
            device_id_type=pl.DeviceIdType.MESH,
        )
    for offset in range(1, groups):
        pl.semaphore_signal(
            barrier, inc=1, device_id=device(here, lax.rem(grp_here + offset, groups)),
            device_id_type=pl.DeviceIdType.MESH,
        )
    pl.semaphore_wait(barrier, len(offsets) + groups - 1)

    inc_ref[...] = msg_ref[...]
    out_ref[:rows] = jnp.zeros((rows, out_ref.shape[1]), jnp.float32)
    out_ref[rows:] = jnp.ones((8, out_ref.shape[1]), jnp.float32)
    for r, d in enumerate(_hops(peers)):
        target = device(lax.rem(here + d, peers), grp_here)
        out_state[r] = inc_ref[:rows].astype(out_state.dtype)
        state_copy = pltpu.make_async_remote_copy(
            src_ref=out_state.at[r],
            dst_ref=recv_state.at[r],
            send_sem=send_sem.at[r],
            recv_sem=recv_sem.at[r],
            device_id=target,
            device_id_type=pl.DeviceIdType.MESH,
        )
        decay_copy = pltpu.make_async_remote_copy(
            src_ref=inc_ref.at[pl.ds(rows, 8)],
            dst_ref=recv_decay.at[r],
            send_sem=decay_send.at[r],
            recv_sem=decay_recv.at[r],
            device_id=target,
            device_id_type=pl.DeviceIdType.MESH,
        )
        state_copy.start()
        decay_copy.start()
        state_copy.wait()
        decay_copy.wait()
        reached = here >= d
        for ref in ((out_ref, inc_ref) if 2 * d < peers else (out_ref,)):
            decay = ref[rows:rows + 1, :]
            for h in range(heads):
                part = pl.ds(h * HP, HP)
                own = ref[part, :]
                got = recv_state[r, part, :].astype(jnp.float32)
                ref[part, :] = jnp.where(reached, decay[:, h:h + 1] * got + own, own)
            ref[rows:] = jnp.where(reached, ref[rows:] * recv_decay[r], ref[rows:])

    send_ref[:rows] = out_ref[:rows].astype(send_ref.dtype)
    send_ref[rows:] = scale_ref[...]
    spread_ref[grp_here] = send_ref[...]
    partner = grp_here + 1 - 2 * lax.rem(grp_here, 2)

    def spread_copy(slot, target, sem):
        return pltpu.make_async_remote_copy(
            src_ref=send_ref if slot is None else spread_ref.at[slot],
            dst_ref=spread_ref.at[grp_here if slot is None else slot],
            send_sem=sem,
            recv_sem=spread_recv.at[grp_here if slot is None else slot],
            device_id=device(here, target),
            device_id_type=pl.DeviceIdType.MESH,
        )

    def arriving(slot, source):
        return pltpu.make_async_remote_copy(
            src_ref=send_ref,
            dst_ref=spread_ref.at[slot],
            send_sem=spread_send.at[0],
            recv_sem=spread_recv.at[slot],
            device_id=device(here, source),
            device_id_type=pl.DeviceIdType.MESH,
        )

    chips = groups // 2
    copies = [spread_copy(None, partner, spread_send.at[0])]
    for k in range(1, chips):
        copies.append(spread_copy(None, lax.rem(grp_here + 2 * k, groups), spread_send.at[k]))
    for copy in copies:
        copy.start()
    arriving(partner, partner).wait_recv()
    forwards = []
    for k in range(1, chips):
        source = lax.rem(grp_here + groups - 2 * k, groups)
        arriving(source, source).wait_recv()
        forward = spread_copy(source, partner, spread_send.at[chips - 1 + k])
        forward.start()
        forwards.append(forward)
    for k in range(1, chips):
        slot = lax.rem(partner + groups - 2 * k, groups)
        arriving(slot, partner).wait_recv()
    for copy in copies + forwards:
        copy.wait_send()


def _hops(peers):
    d, hops = 1, []
    while d < peers:
        hops.append(d)
        d *= 2
    return hops


def carry_in(total_log, state_t, names, after, scale_packed):
    peers = lax.axis_size("seq")
    groups = lax.axis_size("grp")
    heads, width, lanes = state_t.shape
    rows = heads * width
    decay = jnp.ones((8, lanes), jnp.float32).at[0, :heads].set(jnp.exp(total_log))
    msg = jnp.concatenate([state_t.reshape(rows, lanes), decay], axis=0)
    shape = msg.shape
    hops = len(_hops(peers))
    _, spread = pl.pallas_call(
        functools.partial(scan_kernel, peers, names),
        out_shape=(
            jax.ShapeDtypeStruct(shape, jnp.float32),
            jax.ShapeDtypeStruct((groups, rows + scale_packed.shape[0], lanes), jnp.bfloat16),
        ),
        in_specs=[
            pl.BlockSpec(memory_space=pltpu.VMEM),
            pl.BlockSpec(memory_space=pl.ANY),
            pl.BlockSpec(memory_space=pltpu.VMEM),
        ],
        out_specs=(pl.BlockSpec(memory_space=pltpu.VMEM), pl.BlockSpec(memory_space=pltpu.VMEM)),
        scratch_shapes=[
            pltpu.VMEM(shape, jnp.float32),
            pltpu.VMEM((hops, rows, lanes), jnp.bfloat16),
            pltpu.VMEM((hops, rows, lanes), jnp.bfloat16),
            pltpu.VMEM((hops, 8, lanes), jnp.float32),
            pltpu.VMEM((rows + scale_packed.shape[0], lanes), jnp.bfloat16),
            pltpu.SemaphoreType.DMA((hops,)),
            pltpu.SemaphoreType.DMA((hops,)),
            pltpu.SemaphoreType.DMA((hops,)),
            pltpu.SemaphoreType.DMA((hops,)),
            pltpu.SemaphoreType.DMA((groups,)),
            pltpu.SemaphoreType.DMA((groups,)),
        ],
        compiler_params=pltpu.CompilerParams(collective_id=0, has_side_effects=True),
        cost_estimate=pl.CostEstimate(flops=0, transcendentals=0, bytes_accessed=512 * msg.size * 4),
    )(msg, after, scale_packed)
    return spread


def on_device(
    names,
    mixer_input, step_sizes, decay_rates, skip_gain, input_basis, output_basis, out_weight
):
    heads_here = step_sizes.shape[0]
    tokens_here = step_sizes.shape[1]
    count = tokens_here // GROUP
    channels = mixer_input.reshape(heads_here, HP, count, GROUP)
    log_decay = -(decay_rates[:, None] * step_sizes).reshape(heads_here, count, GROUP)
    steps_blocked = step_sizes.reshape(heads_here, count, GROUP)
    running = jnp.cumsum(log_decay, axis=2)
    basis_in_blocked = input_basis.reshape(count, GROUP, N)
    basis_out_blocked = output_basis.reshape(count, GROUP, N)
    gram = jnp.einsum(
        "cin,cjn->cij", basis_out_blocked, basis_in_blocked, preferred_element_type=jnp.float32
    )
    rows_index = lax.broadcasted_iota(jnp.int32, (GROUP, GROUP), 0)
    cols_index = lax.broadcasted_iota(jnp.int32, (GROUP, GROUP), 1)
    causal = rows_index >= cols_index
    gaps = running[:, :, :, None] - running[:, :, None, :]
    mixing = jnp.where(
        causal,
        gram[None] * jnp.exp(jnp.where(causal, gaps, 0.0)) * steps_blocked[:, :, None, :],
        0.0,
    ).astype(jnp.bfloat16)
    inner = jnp.einsum("hcij,hpcj->hpci", mixing, channels, preferred_element_type=jnp.float32)
    tail_decay = jnp.exp(running[:, :, -1:] - running) * steps_blocked
    weighted_terms = (basis_in_blocked.astype(jnp.float32)[None] * tail_decay[:, :, :, None]).astype(
        jnp.bfloat16
    )
    summaries = jnp.einsum(
        "hcjn,hpcj->chnp", weighted_terms, channels, preferred_element_type=jnp.float32
    )
    block_sums = jnp.sum(log_decay, axis=2)
    block_cum = jnp.cumsum(block_sums, axis=1)
    log_prefix = block_cum - block_sums
    total_log = block_cum[:, -1]
    entering = [jnp.zeros_like(summaries[0])]
    for c in range(1, count + 1):
        reach = log_prefix[:, c] if c < count else total_log
        term = jnp.zeros_like(summaries[0])
        for earlier in range(c):
            weight = jnp.exp(reach - block_cum[:, earlier])
            term = term + weight[:, None, None] * summaries[earlier]
        entering.append(term)
    final_state = entering[count]
    entering = jnp.stack(entering[:count])
    basis_out_wide = basis_out_blocked.astype(jnp.float32)
    within = jnp.exp(running)[:, None]
    direct = skip_gain[:, None, None, None] * channels.astype(jnp.float32)
    from_local = jnp.einsum(
        "cin,chnp->hpci", basis_out_wide, entering, precision=lax.Precision.HIGHEST
    )
    local = (inner + from_local * within + direct).astype(jnp.bfloat16)
    scale = jnp.exp(running + log_prefix[:, :, None]).reshape(heads_here, tokens_here)
    scale_hi = scale.astype(jnp.bfloat16)
    scale_lo = (scale - scale_hi.astype(jnp.float32)).astype(jnp.bfloat16)
    scale_rows = jnp.concatenate([scale_hi, scale_lo], axis=0)
    scale_packed = scale_rows.reshape(-1, 128)
    local_flat = local.reshape(heads_here * HP, tokens_here)
    local_all = lax.all_gather(local_flat, "grp", axis=0, tiled=True)
    spread = carry_in(total_log, jnp.swapaxes(final_state, 1, 2), names, local_flat, scale_packed)
    result_t = tail(local_all, output_basis, spread, out_weight.T)
    return result_t.T


def tail_kernel(local_ref, basis_ref, carried_ref, scale_ref, weight_ref, out_ref, acc_ref, mixed_ref):
    g = pl.program_id(0)

    @pl.when(g == 0)
    def _():
        acc_ref[...] = jnp.zeros_like(acc_ref)

    pair, base = carried_ref.shape[0], carried_ref.shape[1]
    tokens = mixed_ref.shape[1]
    per = base // HP
    tiles = tokens // 128
    for sub in range(pair):
        carry = lax.dot_general(
            carried_ref[sub], basis_ref[...], (((1,), (1,)), ((), ())),
            preferred_element_type=jnp.float32,
        )
        for h in range(per):
            for k in range(tiles):
                rows = slice(sub * base + h * HP, sub * base + (h + 1) * HP)
                lanes = slice(k * 128, (k + 1) * 128)
                scale = scale_ref[sub, pl.ds(h * tiles + k, 1), :].astype(jnp.float32) + scale_ref[
                    sub, pl.ds((per + h) * tiles + k, 1), :
                ].astype(jnp.float32)
                mixed_ref[rows, lanes] = (
                    local_ref[rows, lanes].astype(jnp.float32)
                    + carry[h * HP : (h + 1) * HP, lanes] * scale
                ).astype(jnp.bfloat16)
    acc_ref[...] += jnp.dot(weight_ref[...], mixed_ref[...], preferred_element_type=jnp.float32)

    @pl.when(g == pl.num_programs(0) - 1)
    def _():
        out_ref[...] = acc_ref[...].astype(out_ref.dtype)


def tail(local_all, basis, spread, weight_t):
    channels, tokens = local_all.shape
    features = weight_t.shape[0]
    groups = lax.axis_size("grp")
    per = channels // groups // HP
    packed = 2 * per * tokens // 128
    pair = 2 if groups % 2 == 0 else 1
    return pl.pallas_call(
        tail_kernel,
        out_shape=jax.ShapeDtypeStruct((features, tokens), jnp.bfloat16),
        grid=(groups // pair,),
        in_specs=[
            pl.BlockSpec((pair * channels // groups, tokens), lambda g: (g, 0)),
            pl.BlockSpec(basis.shape, lambda g: (0, 0)),
            pl.BlockSpec((pair, per * HP, N), lambda g: (g, 0, 0)),
            pl.BlockSpec((pair, packed, N), lambda g: (g, per * HP // packed, 0)),
            pl.BlockSpec((features, pair * per * HP), lambda g: (0, g)),
        ],
        out_specs=pl.BlockSpec((features, tokens), lambda g: (0, 0)),
        scratch_shapes=[
            pltpu.VMEM((features, tokens), jnp.float32),
            pltpu.VMEM((pair * per * HP, tokens), jnp.bfloat16),
        ],
        cost_estimate=pl.CostEstimate(
            flops=2 * tokens * per * HP * groups * (N + features),
            transcendentals=0,
            bytes_accessed=2 * (local_all.size + weight_t.size) + 2 * features * tokens,
        ),
    )(local_all, basis, spread, spread, weight_t)


def solution(mesh):
    placed = (
        P("grp", "seq"),
        P("grp", "seq"),
        P("grp"),
        P("grp"),
        P("seq", None),
        P("seq", None),
        P(None, "grp"),
    )
    return jax.shard_map(
        functools.partial(on_device, mesh.axis_names), mesh=mesh, in_specs=placed, out_specs=P("seq", "grp"), check_vma=False
    )
```

```python
import functools

import jax
import jax.numpy as jnp
from jax import lax
from jax.experimental import pallas as pl
from jax.experimental.pallas import tpu as pltpu
from jax.sharding import PartitionSpec as P

HP = 64
N = 128
GROUP = 256


def scan_kernel(peers, names, msg_ref, after_ref, scale_ref, out_ref, spread_ref, inc_ref, out_state, recv_state,
                recv_decay, send_ref, send_sem, recv_sem, decay_send, decay_recv, spread_send, spread_recv):
    here = lax.axis_index("seq")
    grp_here = lax.axis_index("grp")
    groups = spread_ref.shape[0]
    rows = msg_ref.shape[0] - 8
    heads = rows // HP

    def device(seq_at, grp_at):
        return tuple(seq_at if name == "seq" else grp_at for name in names)

    offsets = sorted({d % peers for d in _hops(peers)} | {(-d) % peers for d in _hops(peers)})
    barrier = pltpu.get_barrier_semaphore()
    for offset in offsets:
        pl.semaphore_signal(
            barrier, inc=1, device_id=device(lax.rem(here + offset, peers), grp_here),
            device_id_type=pl.DeviceIdType.MESH,
        )
    for offset in range(1, groups):
        pl.semaphore_signal(
            barrier, inc=1, device_id=device(here, lax.rem(grp_here + offset, groups)),
            device_id_type=pl.DeviceIdType.MESH,
        )
    pl.semaphore_wait(barrier, len(offsets) + groups - 1)

    inc_ref[...] = msg_ref[...]
    out_ref[:rows] = jnp.zeros((rows, out_ref.shape[1]), jnp.float32)
    out_ref[rows:] = jnp.ones((8, out_ref.shape[1]), jnp.float32)
    for r, d in enumerate(_hops(peers)):
        target = device(lax.rem(here + d, peers), grp_here)
        out_state[r] = inc_ref[:rows].astype(out_state.dtype)
        state_copy = pltpu.make_async_remote_copy(
            src_ref=out_state.at[r],
            dst_ref=recv_state.at[r],
            send_sem=send_sem.at[r],
            recv_sem=recv_sem.at[r],
            device_id=target,
            device_id_type=pl.DeviceIdType.MESH,
        )
        decay_copy = pltpu.make_async_remote_copy(
            src_ref=inc_ref.at[pl.ds(rows, 8)],
            dst_ref=recv_decay.at[r],
            send_sem=decay_send.at[r],
            recv_sem=decay_recv.at[r],
            device_id=target,
            device_id_type=pl.DeviceIdType.MESH,
        )
        state_copy.start()
        decay_copy.start()
        state_copy.wait()
        decay_copy.wait()
        reached = here >= d
        for ref in ((out_ref, inc_ref) if 2 * d < peers else (out_ref,)):
            decay = ref[rows:rows + 1, :]
            for h in range(heads):
                part = pl.ds(h * HP, HP)
                own = ref[part, :]
                got = recv_state[r, part, :].astype(jnp.float32)
                ref[part, :] = jnp.where(reached, decay[:, h:h + 1] * got + own, own)
            ref[rows:] = jnp.where(reached, ref[rows:] * recv_decay[r], ref[rows:])

    send_ref[:rows] = out_ref[:rows].astype(send_ref.dtype)
    send_ref[rows:] = scale_ref[...]
    spread_ref[grp_here] = send_ref[...]
    partner = grp_here + 1 - 2 * lax.rem(grp_here, 2)

    def spread_copy(slot, target, sem):
        return pltpu.make_async_remote_copy(
            src_ref=send_ref if slot is None else spread_ref.at[slot],
            dst_ref=spread_ref.at[grp_here if slot is None else slot],
            send_sem=sem,
            recv_sem=spread_recv.at[grp_here if slot is None else slot],
            device_id=device(here, target),
            device_id_type=pl.DeviceIdType.MESH,
        )

    def arriving(slot, source):
        return pltpu.make_async_remote_copy(
            src_ref=send_ref,
            dst_ref=spread_ref.at[slot],
            send_sem=spread_send.at[0],
            recv_sem=spread_recv.at[slot],
            device_id=device(here, source),
            device_id_type=pl.DeviceIdType.MESH,
        )

    chips = groups // 2
    copies = [spread_copy(None, partner, spread_send.at[0])]
    for k in range(1, chips):
        copies.append(spread_copy(None, lax.rem(grp_here + 2 * k, groups), spread_send.at[k]))
    for copy in copies:
        copy.start()
    arriving(partner, partner).wait_recv()
    forwards = []
    for k in range(1, chips):
        source = lax.rem(grp_here + groups - 2 * k, groups)
        arriving(source, source).wait_recv()
        forward = spread_copy(source, partner, spread_send.at[chips - 1 + k])
        forward.start()
        forwards.append(forward)
    for k in range(1, chips):
        slot = lax.rem(partner + groups - 2 * k, groups)
        arriving(slot, partner).wait_recv()
    for copy in copies + forwards:
        copy.wait_send()


def _hops(peers):
    d, hops = 1, []
    while d < peers:
        hops.append(d)
        d *= 2
    return hops


def carry_in(total_log, state_t, names, after, scale_packed):
    peers = lax.axis_size("seq")
    groups = lax.axis_size("grp")
    heads, width, lanes = state_t.shape
    rows = heads * width
    decay = jnp.ones((8, lanes), jnp.float32).at[0, :heads].set(jnp.exp(total_log))
    msg = jnp.concatenate([state_t.reshape(rows, lanes), decay], axis=0)
    shape = msg.shape
    hops = len(_hops(peers))
    _, spread = pl.pallas_call(
        functools.partial(scan_kernel, peers, names),
        out_shape=(
            jax.ShapeDtypeStruct(shape, jnp.float32),
            jax.ShapeDtypeStruct((groups, rows + scale_packed.shape[0], lanes), jnp.bfloat16),
        ),
        in_specs=[
            pl.BlockSpec(memory_space=pltpu.VMEM),
            pl.BlockSpec(memory_space=pl.ANY),
            pl.BlockSpec(memory_space=pltpu.VMEM),
        ],
        out_specs=(pl.BlockSpec(memory_space=pltpu.VMEM), pl.BlockSpec(memory_space=pltpu.VMEM)),
        scratch_shapes=[
            pltpu.VMEM(shape, jnp.float32),
            pltpu.VMEM((hops, rows, lanes), jnp.bfloat16),
            pltpu.VMEM((hops, rows, lanes), jnp.bfloat16),
            pltpu.VMEM((hops, 8, lanes), jnp.float32),
            pltpu.VMEM((rows + scale_packed.shape[0], lanes), jnp.bfloat16),
            pltpu.SemaphoreType.DMA((hops,)),
            pltpu.SemaphoreType.DMA((hops,)),
            pltpu.SemaphoreType.DMA((hops,)),
            pltpu.SemaphoreType.DMA((hops,)),
            pltpu.SemaphoreType.DMA((groups,)),
            pltpu.SemaphoreType.DMA((groups,)),
        ],
        compiler_params=pltpu.CompilerParams(collective_id=0, has_side_effects=True),
        cost_estimate=pl.CostEstimate(flops=0, transcendentals=0, bytes_accessed=512 * msg.size * 4),
    )(msg, after, scale_packed)
    return spread


def on_device(
    names,
    mixer_input, step_sizes, decay_rates, skip_gain, input_basis, output_basis, out_weight
):
    heads_here = step_sizes.shape[0]
    tokens_here = step_sizes.shape[1]
    count = tokens_here // GROUP
    channels = mixer_input.reshape(heads_here, HP, count, GROUP)
    log_decay = -(decay_rates[:, None] * step_sizes).reshape(heads_here, count, GROUP)
    steps_blocked = step_sizes.reshape(heads_here, count, GROUP)
    running = jnp.cumsum(log_decay, axis=2)
    basis_in_blocked = input_basis.reshape(count, GROUP, N)
    basis_out_blocked = output_basis.reshape(count, GROUP, N)
    gram = jnp.einsum(
        "cin,cjn->cij", basis_out_blocked, basis_in_blocked, preferred_element_type=jnp.float32
    )
    rows_index = lax.broadcasted_iota(jnp.int32, (GROUP, GROUP), 0)
    cols_index = lax.broadcasted_iota(jnp.int32, (GROUP, GROUP), 1)
    causal = rows_index >= cols_index
    gaps = running[:, :, :, None] - running[:, :, None, :]
    mixing = jnp.where(
        causal,
        gram[None] * jnp.exp(jnp.where(causal, gaps, 0.0)) * steps_blocked[:, :, None, :],
        0.0,
    ).astype(jnp.bfloat16)
    inner = jnp.einsum("hcij,hpcj->hpci", mixing, channels, preferred_element_type=jnp.float32)
    tail_decay = jnp.exp(running[:, :, -1:] - running) * steps_blocked
    weighted_terms = (basis_in_blocked.astype(jnp.float32)[None] * tail_decay[:, :, :, None]).astype(
        jnp.bfloat16
    )
    summaries = jnp.einsum(
        "hcjn,hpcj->chnp", weighted_terms, channels, preferred_element_type=jnp.float32
    )
    block_sums = jnp.sum(log_decay, axis=2)
    block_cum = jnp.cumsum(block_sums, axis=1)
    log_prefix = block_cum - block_sums
    total_log = block_cum[:, -1]
    entering = [jnp.zeros_like(summaries[0])]
    for c in range(1, count + 1):
        reach = log_prefix[:, c] if c < count else total_log
        term = jnp.zeros_like(summaries[0])
        for earlier in range(c):
            weight = jnp.exp(reach - block_cum[:, earlier])
            term = term + weight[:, None, None] * summaries[earlier]
        entering.append(term)
    final_state = entering[count]
    entering = jnp.stack(entering[:count])
    basis_out_wide = basis_out_blocked.astype(jnp.float32)
    within = jnp.exp(running)[:, None]
    direct = skip_gain[:, None, None, None] * channels.astype(jnp.float32)
    from_local = jnp.einsum(
        "cin,chnp->hpci", basis_out_wide, entering, precision=lax.Precision.HIGHEST
    )
    local = (inner + from_local * within + direct).astype(jnp.bfloat16)
    scale = jnp.exp(running + log_prefix[:, :, None]).reshape(heads_here, tokens_here)
    scale_hi = scale.astype(jnp.bfloat16)
    scale_lo = (scale - scale_hi.astype(jnp.float32)).astype(jnp.bfloat16)
    scale_rows = jnp.concatenate([scale_hi, scale_lo], axis=0)
    scale_packed = scale_rows.reshape(-1, 128)
    local_flat = local.reshape(heads_here * HP, tokens_here)
    local_all = lax.all_gather(local_flat, "grp", axis=0, tiled=True)
    spread = carry_in(total_log, jnp.swapaxes(final_state, 1, 2), names, local_flat, scale_packed)
    result_t = tail(local_all, output_basis, spread, out_weight.T)
    return result_t.T


def tail_kernel(local_ref, basis_ref, carried_ref, scale_ref, weight_ref, out_ref, acc_ref, mixed_ref):
    g = pl.program_id(0)

    @pl.when(g == 0)
    def _():
        acc_ref[...] = jnp.zeros_like(acc_ref)

    pair, base = carried_ref.shape[0], carried_ref.shape[1]
    tokens = mixed_ref.shape[1]
    per = base // HP
    tiles = tokens // 128
    for sub in range(pair):
        carry = lax.dot_general(
            carried_ref[sub], basis_ref[...], (((1,), (1,)), ((), ())),
            preferred_element_type=jnp.float32,
        )
        for h in range(per):
            for k in range(tiles):
                rows = slice(sub * base + h * HP, sub * base + (h + 1) * HP)
                lanes = slice(k * 128, (k + 1) * 128)
                scale = scale_ref[sub, pl.ds(h * tiles + k, 1), :].astype(jnp.float32) + scale_ref[
                    sub, pl.ds((per + h) * tiles + k, 1), :
                ].astype(jnp.float32)
                mixed_ref[rows, lanes] = (
                    local_ref[rows, lanes].astype(jnp.float32)
                    + carry[h * HP : (h + 1) * HP, lanes] * scale
                ).astype(jnp.bfloat16)
    acc_ref[...] += jnp.dot(weight_ref[...], mixed_ref[...], preferred_element_type=jnp.float32)

    @pl.when(g == pl.num_programs(0) - 1)
    def _():
        out_ref[...] = acc_ref[...].astype(out_ref.dtype)


def tail(local_all, basis, spread, weight_t):
    channels, tokens = local_all.shape
    features = weight_t.shape[0]
    groups = lax.axis_size("grp")
    per = channels // groups // HP
    packed = 2 * per * tokens // 128
    pair = 4 if groups % 4 == 0 else 1
    return pl.pallas_call(
        tail_kernel,
        out_shape=jax.ShapeDtypeStruct((features, tokens), jnp.bfloat16),
        grid=(groups // pair,),
        in_specs=[
            pl.BlockSpec((pair * channels // groups, tokens), lambda g: (g, 0)),
            pl.BlockSpec(basis.shape, lambda g: (0, 0)),
            pl.BlockSpec((pair, per * HP, N), lambda g: (g, 0, 0)),
            pl.BlockSpec((pair, packed, N), lambda g: (g, per * HP // packed, 0)),
            pl.BlockSpec((features, pair * per * HP), lambda g: (0, g)),
        ],
        out_specs=pl.BlockSpec((features, tokens), lambda g: (0, 0)),
        scratch_shapes=[
            pltpu.VMEM((features, tokens), jnp.float32),
            pltpu.VMEM((pair * per * HP, tokens), jnp.bfloat16),
        ],
        cost_estimate=pl.CostEstimate(
            flops=2 * tokens * per * HP * groups * (N + features),
            transcendentals=0,
            bytes_accessed=2 * (local_all.size + weight_t.size) + 2 * features * tokens,
        ),
    )(local_all, basis, spread, spread, weight_t)


def solution(mesh):
    placed = (
        P("grp", "seq"),
        P("grp", "seq"),
        P("grp"),
        P("grp"),
        P("seq", None),
        P("seq", None),
        P(None, "grp"),
    )
    return jax.shard_map(
        functools.partial(on_device, mesh.axis_names), mesh=mesh, in_specs=placed, out_specs=P("seq", "grp"), check_vma=False
    )
```
